512 devices in a mesh: row: 32 (over y, x), col: 16 (over z, core).
Axes of the slice: x: 4, y: 8, z: 8, core: 2. Of those that a mesh axis runs over, the one named last changes fastest.
Arguments:
- blocks: bfloat16 [32, 16, 2, 8, 128, 128], P('row', 'col'), may hold values from -4 to 4
- block_rows: int32 [32, 16, 2, 8], P('row', 'col'), may hold values from 0 to 4, as said below
- block_cols: int32 [32, 16, 2, 8], P('row', 'col'), may hold values from 0 to 4, as said below
- counts: int32 [32, 16, 2], P('row', 'col'), may hold values from 2 to 8, as said below
Outputs:
- square: bfloat16 [20480, 20480], P('row', 'col')
- trace_value: float32 [], replicated
The draws below stay inside these ranges and needn't reach their ends.
Inputs may be any that keep to these rules, and one draw needn't show every extreme that they name: `block_rows`: in every (row panel, column panel, group) the 8 slots name distinct block positions; a slot holds data only if its index is below the group's count. `block_cols`: together with block_rows each slot names a distinct position of the 5 x 5 grid of its group. `counts`: some group is full in every draw.
All inputs are finite; a program needn't handle non-finite values.
Results may differ from the reference program's by a relative error of at most 0.001.
Values may be sent and summed in bfloat16 or wider, within the bound.
A program may use at most 64 MiB of HBM per device.

```python
import math
import jax
import jax.numpy as jnp
from jax import lax

BS = 128
RB = 5
SLOTS = 8
STEPS = 4
G = 2
ORDER = 20480
N_ROW = 32
N_COL = 16


def pattern(key):
    groups = N_ROW // N_COL
    base = jax.random.fold_in(key, 11)
    keys = jax.random.split(base, N_ROW * N_COL * groups)
    perms = jax.vmap(lambda single: jax.random.permutation(single, RB * RB)[:SLOTS])(keys)
    return perms.reshape(N_ROW, N_COL, groups, SLOTS).astype(jnp.int32)


def draw_block_rows(key, part):
    return (pattern(key) // RB).astype(jnp.int32)


def draw_block_cols(key, part):
    return (pattern(key) % RB).astype(jnp.int32)


def draw_counts(key, part):
    groups = N_ROW // N_COL
    total = N_ROW * N_COL * groups
    lowest = max(1, SLOTS // 4)
    first = jax.random.randint(jax.random.fold_in(key, 21), (total,), lowest, SLOTS + 1, dtype=jnp.int32)
    second = jax.random.randint(jax.random.fold_in(key, 22), (total,), lowest, SLOTS + 1, dtype=jnp.int32)
    fullest = jax.random.randint(jax.random.fold_in(key, 23), (), 0, total, dtype=jnp.int32)
    values = jnp.minimum(first, second)
    values = jnp.where(jnp.arange(total, dtype=jnp.int32) == fullest, SLOTS, values)
    return values.reshape(N_ROW, N_COL, groups).astype(jnp.int32)


def shard_levels(key, shape, cuts, smallest, top_value):
    loudness, own = 1.0, jax.random.fold_in(key, 6)
    for axis_at, blocks in cuts:
        steps = jnp.exp(jax.random.uniform(jax.random.fold_in(own, axis_at), (blocks,), jnp.float32, smallest / len(cuts), top_value / len(cuts)))
        loudness = loudness * jnp.repeat(steps, shape[axis_at] // blocks).reshape([-1 if axis == axis_at else 1 for axis in range(len(shape))])
    return loudness


def centred(stream_key, extent, scale, limit, cuts=(), held_as=jnp.bfloat16):
    result = jax.random.normal(stream_key, extent, jnp.float32) * scale
    if len(cuts) > 0:
        result = shard_levels(stream_key, extent, cuts, -0.22, 0.18) * result
    return jnp.clip(result, min=-limit, max=limit).astype(held_as)


def setup_inputs(seed: int = 0) -> dict:
    arg_keys = jax.random.split(jax.random.key(seed), 5)
    blocks = centred(arg_keys[0], (N_ROW, N_COL, G, SLOTS, BS, BS), 0.29, 4.0, ((0, 32), (1, 16)))
    block_rows = draw_block_rows(jax.random.fold_in(arg_keys[4], 71), 0)
    block_cols = draw_block_cols(jax.random.fold_in(arg_keys[4], 71), 0)
    counts = draw_counts(jax.random.fold_in(arg_keys[4], 71), 0)
    return dict(blocks=blocks, block_rows=block_rows, block_cols=block_cols, counts=counts)


def densify(pieces, rows, cols, nrows, ncols):
    width = pieces.shape[-1]
    count = pieces.shape[0]
    places = rows * ncols + cols
    onehot = (places[None, :] == jnp.arange(nrows * ncols, dtype=jnp.int32)[:, None]).astype(pieces.dtype)
    dense = jnp.dot(onehot, pieces.reshape(count, width * width), preferred_element_type=jnp.float32)
    dense = dense.reshape(nrows, ncols, width, width).transpose(0, 2, 1, 3)
    return dense.reshape(nrows * width, ncols * width).astype(pieces.dtype)

def reference(blocks, block_rows, block_cols, counts):
    groups = N_ROW // N_COL
    live = jnp.arange(SLOTS, dtype=jnp.int32)[None, None, None, :] < counts[..., None]
    masked = blocks * live[..., None, None].astype(blocks.dtype)
    offsets = (jnp.arange(groups, dtype=jnp.int32) * RB)[:, None]

    def device(index):
        panel_row = index // N_COL
        panel_col = index % N_COL
        upper = panel_row // groups
        lower = panel_row % groups
        totals = jnp.zeros((RB * BS, groups * RB * BS), jnp.float32)
        for step in range(STEPS):
            source_col = (panel_col + step + upper) % N_COL
            part = groups * source_col + lower
            left = densify(masked[panel_row, source_col, lower], block_rows[panel_row, source_col, lower], block_cols[panel_row, source_col, lower], RB, RB)
            right = densify(masked[part, panel_col].reshape(groups * SLOTS, BS, BS), block_rows[part, panel_col].reshape(-1), (block_cols[part, panel_col] + offsets).reshape(-1), RB, groups * RB)
            totals = totals + jnp.dot(left, right, preferred_element_type=jnp.float32)
        shift_amount = panel_row - groups * panel_col
        valid = (shift_amount >= 0) & (shift_amount < groups)
        start = (jnp.clip(shift_amount, 0, groups - 1) * RB * BS).astype(jnp.int32)
        window = lax.dynamic_slice_in_dim(totals, start, RB * BS, 1)
        term = jnp.where(valid, jnp.trace(window), jnp.zeros((), jnp.float32))
        return (totals.astype(jnp.bfloat16), term)
    panels, terms = lax.map(device, jnp.arange(N_ROW * N_COL, dtype=jnp.int32))
    square = panels.reshape(N_ROW, N_COL, RB * BS, groups * RB * BS).transpose(0, 2, 1, 3)
    square = square.reshape(N_ROW * RB * BS, N_COL * groups * RB * BS)
    trace_value = jnp.sum(terms) / math.sqrt(ORDER)
    return (square, trace_value)
```

```python
import math

import jax
import jax.numpy as jnp
from jax import lax
from jax.sharding import PartitionSpec as P

RB = 5
STEPS = 4


def densify(pieces, places, nrows, ncols):
    width = pieces.shape[-1]
    count = pieces.shape[0]
    onehot = (places[None, :] == jnp.arange(nrows * ncols, dtype=jnp.int32)[:, None]).astype(
        pieces.dtype
    )
    dense = jnp.dot(
        onehot, pieces.reshape(count, width * width), preferred_element_type=jnp.float32
    )
    dense = dense.reshape(nrows, ncols, width, width).transpose(0, 2, 1, 3)
    return dense.reshape(nrows * width, ncols * width).astype(pieces.dtype)


def fetch(value, source_of, row_count, col_count):
    pairs = []
    for r in range(row_count):
        for c in range(col_count):
            sr, sc = source_of(r, c)
            pairs.append((sr * col_count + sc, r * col_count + c))
    return lax.ppermute(value, ("row", "col"), pairs)


def body(blocks, block_rows, block_cols, counts):
    groups = blocks.shape[2]
    slot_count = blocks.shape[3]
    width = blocks.shape[4]
    row_count = lax.axis_size("row")
    col_count = lax.axis_size("col")
    row_place = lax.axis_index("row")
    col_place = lax.axis_index("col")
    lower = row_place % groups
    filled = counts[0, 0]
    live = jnp.arange(slot_count, dtype=jnp.int32)[None, :] < filled[:, None]
    left_places_all = jnp.where(live, block_rows[0, 0] * RB + block_cols[0, 0], -1)
    offsets = (jnp.arange(groups, dtype=jnp.int32) * RB)[:, None]
    right_places = jnp.where(
        live, block_rows[0, 0] * (groups * RB) + block_cols[0, 0] + offsets, -1
    ).reshape(-1)
    left_pieces = lax.dynamic_index_in_dim(blocks[0, 0], lower, 0, keepdims=False)
    left_places = lax.dynamic_index_in_dim(left_places_all, lower, 0, keepdims=False)
    right_pieces = blocks[0, 0].reshape(groups * slot_count, width, width)
    totals = jnp.zeros((RB * width, groups * RB * width), jnp.float32)
    for step in range(STEPS):
        def left_source(r, c, step=step):
            return r, (c + r // groups + step) % col_count

        def right_source(r, c, step=step):
            return (r + groups * c + groups * step) % row_count, c

        lp = fetch(left_pieces, left_source, row_count, col_count)
        lq = fetch(left_places, left_source, row_count, col_count)
        rp = fetch(right_pieces, right_source, row_count, col_count)
        rq = fetch(right_places, right_source, row_count, col_count)
        right_dense = densify(rp, rq, RB, groups * RB)
        left_dense = densify(lp, lq, RB, RB)
        totals = totals + jnp.dot(left_dense, right_dense, preferred_element_type=jnp.float32)
    shift_amount = row_place - groups * col_place
    valid = (shift_amount >= 0) & (shift_amount < groups)
    start = jnp.clip(shift_amount, 0, groups - 1) * RB * width
    window = lax.dynamic_slice_in_dim(totals, start, RB * width, 1)
    term = jnp.where(valid, jnp.trace(window), jnp.zeros((), jnp.float32))
    overall = lax.psum(lax.psum(term, "col"), "row")
    trace_value = overall / math.sqrt(row_count * RB * width)
    return (totals.astype(jnp.bfloat16), trace_value)


def solution(mesh):
    return jax.shard_map(
        body,
        mesh=mesh,
        in_specs=(
            P("row", "col", None, None, None, None),
            P("row", "col", None, None),
            P("row", "col", None, None),
            P("row", "col", None),
        ),
        out_specs=(P("row", "col"), P()),
        check_vma=False,
    )
```

```python
import functools
import math

import jax
import jax.numpy as jnp
from jax import lax
from jax.experimental import pallas as pl
from jax.experimental.pallas import tpu as pltpu
from jax.sharding import PartitionSpec as P

RB = 5
STEPS = 4
MESH = pl.DeviceIdType.MESH


def densify(pieces, places, nrows, ncols):
    width = pieces.shape[-1]
    count = pieces.shape[0]
    onehot = (places[None, :] == jnp.arange(nrows * ncols, dtype=jnp.int32)[:, None]).astype(
        pieces.dtype
    )
    dense = jnp.dot(
        onehot, pieces.reshape(count, width * width), preferred_element_type=jnp.float32
    )
    dense = dense.reshape(nrows, ncols, width, width).transpose(0, 2, 1, 3)
    return dense.reshape(nrows * width, ncols * width).astype(pieces.dtype)


def exchange_kernel(row_count, col_count, groups,
                    blocks_ref, meta_ref, recv_l, recv_r, recv_ml, recv_mr, send_sem, recv_sem):
    r = lax.axis_index("row")
    c = lax.axis_index("col")
    a = r // groups
    b = r % groups
    plans = []
    for s in range(STEPS):
        l_self = (a + s) % col_count == 0
        l_dst = (r, (c - a - s + 2 * col_count) % col_count)
        l_src = (r, (c + a + s) % col_count)
        r_self = (c + s) % col_count == 0
        r_dst = ((r - groups * (c + s) + 2 * row_count) % row_count, c)
        r_src = ((r + groups * (c + s)) % row_count, c)
        plans.append((l_self, l_dst, l_src, r_self, r_dst, r_src))

    barrier = pltpu.get_barrier_semaphore()
    for l_self, l_dst, l_src, r_self, r_dst, r_src in plans:
        for is_self, dst, src in ((l_self, l_dst, l_src), (r_self, r_dst, r_src)):
            @pl.when(jnp.logical_not(is_self))
            def _(dst=dst, src=src):
                pl.semaphore_signal(barrier, 1, device_id=dst, device_id_type=MESH)
                pl.semaphore_signal(barrier, 1, device_id=src, device_id_type=MESH)
    peers = 0
    for l_self, l_dst, l_src, r_self, r_dst, r_src in plans:
        for is_self in (l_self, r_self):
            peers = peers + jnp.where(is_self, 0, 2)
    pl.semaphore_wait(barrier, peers)

    copies = []
    for s, (l_self, l_dst, l_src, r_self, r_dst, r_src) in enumerate(plans):
        jobs = (
            (l_self, l_dst, blocks_ref.at[b], recv_l.at[s], 4 * s),
            (l_self, l_dst, meta_ref, recv_ml.at[s], 4 * s + 1),
            (r_self, r_dst, blocks_ref, recv_r.at[s], 4 * s + 2),
            (r_self, r_dst, meta_ref, recv_mr.at[s], 4 * s + 3),
        )
        for is_self, dst, src_ref, dst_ref, k in jobs:
            local = pltpu.make_async_copy(src_ref, dst_ref, recv_sem.at[k])
            remote = pltpu.make_async_remote_copy(
                src_ref, dst_ref, send_sem.at[k], recv_sem.at[k],
                device_id=dst, device_id_type=MESH,
            )
            copies.append((is_self, local, remote))

            @pl.when(is_self)
            def _(local=local):
                local.start()

            @pl.when(jnp.logical_not(is_self))
            def _(remote=remote):
                remote.start()

    for is_self, local, remote in copies:
        @pl.when(is_self)
        def _(local=local):
            local.wait()

        @pl.when(jnp.logical_not(is_self))
        def _(remote=remote):
            remote.wait_send()
            remote.wait_recv()


def exchange(blocks, meta, row_count, col_count):
    groups, slots, width = blocks.shape[0], blocks.shape[1], blocks.shape[2]
    vmem = pl.BlockSpec(memory_space=pltpu.VMEM)
    return pl.pallas_call(
        functools.partial(exchange_kernel, row_count, col_count, groups),
        out_shape=(
            jax.ShapeDtypeStruct((STEPS, slots, width, width), blocks.dtype),
            jax.ShapeDtypeStruct((STEPS, groups, slots, width, width), blocks.dtype),
            jax.ShapeDtypeStruct((STEPS,) + meta.shape, meta.dtype),
            jax.ShapeDtypeStruct((STEPS,) + meta.shape, meta.dtype),
        ),
        in_specs=[vmem, vmem],
        out_specs=(vmem, vmem, vmem, vmem),
        scratch_shapes=[
            pltpu.SemaphoreType.DMA((4 * STEPS,)),
            pltpu.SemaphoreType.DMA((4 * STEPS,)),
        ],
        compiler_params=pltpu.CompilerParams(collective_id=0, has_side_effects=True),
    )(blocks, meta)


def body(blocks, block_rows, block_cols, counts):
    groups = blocks.shape[2]
    slot_count = blocks.shape[3]
    width = blocks.shape[4]
    row_count = lax.axis_size("row")
    col_count = lax.axis_size("col")
    row_place = lax.axis_index("row")
    col_place = lax.axis_index("col")
    lower = row_place % groups
    filled = counts[0, 0]
    live = jnp.arange(slot_count, dtype=jnp.int32)[None, :] < filled[:, None]
    left_places_all = jnp.where(live, block_rows[0, 0] * RB + block_cols[0, 0], -1)
    offsets = (jnp.arange(groups, dtype=jnp.int32) * RB)[:, None]
    right_places = jnp.where(
        live, block_rows[0, 0] * (groups * RB) + block_cols[0, 0] + offsets, -1
    ).reshape(-1)
    left_places = lax.dynamic_index_in_dim(left_places_all, lower, 0, keepdims=False)
    meta = jnp.zeros((8, 128), jnp.int32)
    meta = meta.at[0, :slot_count].set(left_places)
    meta = meta.at[1, : groups * slot_count].set(right_places)
    recv_l, recv_r, recv_ml, recv_mr = exchange(blocks[0, 0], meta, row_count, col_count)
    totals = jnp.zeros((RB * width, groups * RB * width), jnp.float32)
    for step in range(STEPS):
        rp = recv_r[step].reshape(groups * slot_count, width, width)
        right_dense = densify(rp, recv_mr[step, 1, : groups * slot_count], RB, groups * RB)
        left_dense = densify(recv_l[step], recv_ml[step, 0, :slot_count], RB, RB)
        totals = totals + jnp.dot(left_dense, right_dense, preferred_element_type=jnp.float32)
    shift_amount = row_place - groups * col_place
    valid = (shift_amount >= 0) & (shift_amount < groups)
    start = jnp.clip(shift_amount, 0, groups - 1) * RB * width
    window = lax.dynamic_slice_in_dim(totals, start, RB * width, 1)
    term = jnp.where(valid, jnp.trace(window), jnp.zeros((), jnp.float32))
    overall = lax.psum(lax.psum(term, "col"), "row")
    trace_value = overall / math.sqrt(row_count * RB * width)
    return (totals.astype(jnp.bfloat16), trace_value)


def solution(mesh):
    return jax.shard_map(
        body,
        mesh=mesh,
        in_specs=(
            P("row", "col", None, None, None, None),
            P("row", "col", None, None),
            P("row", "col", None, None),
            P("row", "col", None),
        ),
        out_specs=(P("row", "col"), P()),
        check_vma=False,
    )
```

```python
import functools
import math

import jax
import jax.numpy as jnp
from jax import lax
from jax.experimental import pallas as pl
from jax.experimental.pallas import tpu as pltpu
from jax.sharding import PartitionSpec as P

RB = 5
STEPS = 4
MESH = pl.DeviceIdType.MESH


def densify(pieces, places, nrows, ncols):
    width = pieces.shape[-1]
    count = pieces.shape[0]
    onehot = (places[None, :] == jnp.arange(nrows * ncols, dtype=jnp.int32)[:, None]).astype(
        pieces.dtype
    )
    dense = jnp.dot(
        onehot, pieces.reshape(count, width * width), preferred_element_type=jnp.float32
    )
    dense = dense.reshape(nrows, ncols, width, width).transpose(0, 2, 1, 3)
    return dense.reshape(nrows * width, ncols * width).astype(pieces.dtype)


def exchange_kernel(row_count, col_count, groups,
                    blocks_ref, meta_ref, recv_l, recv_r, recv_ml, recv_mr, send_sem, recv_sem):
    r = lax.axis_index("row")
    c = lax.axis_index("col")
    a = r // groups
    b = r % groups
    plans = []
    for s in range(STEPS):
        l_self = (a + s) % col_count == 0
        l_dst = (r, (c - a - s + 2 * col_count) % col_count)
        l_src = (r, (c + a + s) % col_count)
        r_self = (c + s) % col_count == 0
        r_dst = ((r - groups * (c + s) + 2 * row_count) % row_count, c)
        r_src = ((r + groups * (c + s)) % row_count, c)
        plans.append((l_self, l_dst, l_src, r_self, r_dst, r_src))

    barrier = pltpu.get_barrier_semaphore()
    for l_self, l_dst, l_src, r_self, r_dst, r_src in plans:
        for is_self, dst, src in ((l_self, l_dst, l_src), (r_self, r_dst, r_src)):
            @pl.when(jnp.logical_not(is_self))
            def _(dst=dst, src=src):
                pl.semaphore_signal(barrier, 1, device_id=dst, device_id_type=MESH)
                pl.semaphore_signal(barrier, 1, device_id=src, device_id_type=MESH)
    peers = 0
    for l_self, l_dst, l_src, r_self, r_dst, r_src in plans:
        for is_self in (l_self, r_self):
            peers = peers + jnp.where(is_self, 0, 2)
    pl.semaphore_wait(barrier, peers)

    copies = []
    for s, (l_self, l_dst, l_src, r_self, r_dst, r_src) in enumerate(plans):
        jobs = (
            (l_self, l_dst, blocks_ref.at[b], recv_l.at[s], 4 * s),
            (l_self, l_dst, meta_ref, recv_ml.at[s], 4 * s + 1),
            (r_self, r_dst, blocks_ref, recv_r.at[s], 4 * s + 2),
            (r_self, r_dst, meta_ref, recv_mr.at[s], 4 * s + 3),
        )
        for is_self, dst, src_ref, dst_ref, k in jobs:
            local = pltpu.make_async_copy(src_ref, dst_ref, recv_sem.at[k])
            remote = pltpu.make_async_remote_copy(
                src_ref, dst_ref, send_sem.at[k], recv_sem.at[k],
                device_id=dst, device_id_type=MESH,
            )
            copies.append((is_self, local, remote))

            @pl.when(is_self)
            def _(local=local):
                local.start()

            @pl.when(jnp.logical_not(is_self))
            def _(remote=remote):
                remote.start()

    for is_self, local, remote in copies:
        @pl.when(is_self)
        def _(local=local):
            local.wait()

        @pl.when(jnp.logical_not(is_self))
        def _(remote=remote):
            remote.wait_send()
            remote.wait_recv()


def exchange(blocks, meta, row_count, col_count):
    groups, slots, width = blocks.shape[0], blocks.shape[1], blocks.shape[2]
    vmem = pl.BlockSpec(memory_space=pltpu.VMEM)
    return pl.pallas_call(
        functools.partial(exchange_kernel, row_count, col_count, groups),
        out_shape=(
            jax.ShapeDtypeStruct((STEPS, slots, width, width), blocks.dtype),
            jax.ShapeDtypeStruct((STEPS, groups, slots, width, width), blocks.dtype),
            jax.ShapeDtypeStruct((STEPS,) + meta.shape, meta.dtype),
            jax.ShapeDtypeStruct((STEPS,) + meta.shape, meta.dtype),
        ),
        in_specs=[vmem, vmem],
        out_specs=(vmem, vmem, vmem, vmem),
        scratch_shapes=[
            pltpu.SemaphoreType.DMA((4 * STEPS,)),
            pltpu.SemaphoreType.DMA((4 * STEPS,)),
        ],
        compiler_params=pltpu.CompilerParams(collective_id=0, has_side_effects=True),
    )(blocks, meta)


def trace_kernel(row_count, col_count, groups,
                 term_ref, out_ref, row_buf, col_buf, send_sem, recv_sem, col_send, col_recv):
    r = lax.axis_index("row")
    c = lax.axis_index("col")
    diagonal = c == r // groups
    barrier = pltpu.get_barrier_semaphore()

    @pl.when(diagonal)
    def _():
        for cc in range(col_count):
            @pl.when(cc != c)
            def _(cc=cc):
                pl.semaphore_signal(barrier, 1, device_id=(r, cc), device_id_type=MESH)

    @pl.when(jnp.logical_not(diagonal))
    def _():
        pl.semaphore_signal(barrier, 1, device_id=(r, r // groups), device_id_type=MESH)

    for rr in range(row_count):
        @pl.when(rr != r)
        def _(rr=rr):
            pl.semaphore_signal(barrier, 1, device_id=(rr, c), device_id_type=MESH)

    pl.semaphore_wait(barrier, (row_count - 1) + jnp.where(diagonal, col_count - 1, 1))

    row_copies = []
    for cc in range(col_count):
        row_copies.append(pltpu.make_async_remote_copy(
            term_ref, row_buf, send_sem.at[cc], recv_sem.at[0],
            device_id=(r, cc), device_id_type=MESH,
        ))

    @pl.when(diagonal)
    def _():
        for cc in range(col_count):
            @pl.when(cc != c)
            def _(cc=cc):
                row_copies[cc].start()

    @pl.when(jnp.logical_not(diagonal))
    def _():
        row_copies[0].wait_recv()

    def col_copy(source, rr):
        return pltpu.make_async_remote_copy(
            source, col_buf.at[r], col_send.at[rr], col_recv.at[r],
            device_id=(rr, c), device_id_type=MESH,
        )

    for source, chosen in ((term_ref, diagonal), (row_buf, jnp.logical_not(diagonal))):
        @pl.when(chosen)
        def _(source=source):
            for rr in range(row_count):
                @pl.when(rr != r)
                def _(rr=rr):
                    col_copy(source, rr).start()

    for rr in range(row_count):
        @pl.when(rr != r)
        def _(rr=rr):
            pltpu.make_async_remote_copy(
                term_ref, col_buf.at[rr], col_send.at[rr], col_recv.at[rr],
                device_id=(rr, c), device_id_type=MESH,
            ).wait_recv()

    for source, chosen in ((term_ref, diagonal), (row_buf, jnp.logical_not(diagonal))):
        @pl.when(chosen)
        def _(source=source):
            for rr in range(row_count):
                @pl.when(rr != r)
                def _(rr=rr):
                    col_copy(source, rr).wait_send()
            col_buf[r] = source[...]

    @pl.when(diagonal)
    def _():
        for cc in range(col_count):
            @pl.when(cc != c)
            def _(cc=cc):
                row_copies[cc].wait_send()

    total = jnp.zeros(out_ref.shape, jnp.float32)
    for rr in range(row_count):
        total = total + col_buf[rr]
    out_ref[...] = total


def trace_total(term, row_count, col_count, groups):
    tile = jnp.broadcast_to(term, (8, 128))
    vmem = pl.BlockSpec(memory_space=pltpu.VMEM)
    out = pl.pallas_call(
        functools.partial(trace_kernel, row_count, col_count, groups),
        out_shape=jax.ShapeDtypeStruct((8, 128), jnp.float32),
        in_specs=[vmem],
        out_specs=vmem,
        scratch_shapes=[
            pltpu.VMEM((8, 128), jnp.float32),
            pltpu.VMEM((row_count, 8, 128), jnp.float32),
            pltpu.SemaphoreType.DMA((col_count,)),
            pltpu.SemaphoreType.DMA((1,)),
            pltpu.SemaphoreType.DMA((row_count,)),
            pltpu.SemaphoreType.DMA((row_count,)),
        ],
        compiler_params=pltpu.CompilerParams(collective_id=1, has_side_effects=True),
    )(tile)
    return out[0, 0]


def body(blocks, block_rows, block_cols, counts):
    groups = blocks.shape[2]
    slot_count = blocks.shape[3]
    width = blocks.shape[4]
    row_count = lax.axis_size("row")
    col_count = lax.axis_size("col")
    row_place = lax.axis_index("row")
    col_place = lax.axis_index("col")
    lower = row_place % groups
    filled = counts[0, 0]
    live = jnp.arange(slot_count, dtype=jnp.int32)[None, :] < filled[:, None]
    left_places_all = jnp.where(live, block_rows[0, 0] * RB + block_cols[0, 0], -1)
    offsets = (jnp.arange(groups, dtype=jnp.int32) * RB)[:, None]
    right_places = jnp.where(
        live, block_rows[0, 0] * (groups * RB) + block_cols[0, 0] + offsets, -1
    ).reshape(-1)
    left_places = lax.dynamic_index_in_dim(left_places_all, lower, 0, keepdims=False)
    meta = jnp.zeros((8, 128), jnp.int32)
    meta = meta.at[0, :slot_count].set(left_places)
    meta = meta.at[1, : groups * slot_count].set(right_places)
    recv_l, recv_r, recv_ml, recv_mr = exchange(blocks[0, 0], meta, row_count, col_count)
    totals = jnp.zeros((RB * width, groups * RB * width), jnp.float32)
    for step in range(STEPS):
        rp = recv_r[step].reshape(groups * slot_count, width, width)
        right_dense = densify(rp, recv_mr[step, 1, : groups * slot_count], RB, groups * RB)
        left_dense = densify(recv_l[step], recv_ml[step, 0, :slot_count], RB, RB)
        totals = totals + jnp.dot(left_dense, right_dense, preferred_element_type=jnp.float32)
    shift_amount = row_place - groups * col_place
    valid = (shift_amount >= 0) & (shift_amount < groups)
    start = jnp.clip(shift_amount, 0, groups - 1) * RB * width
    window = lax.dynamic_slice_in_dim(totals, start, RB * width, 1)
    term = jnp.where(valid, jnp.trace(window), jnp.zeros((), jnp.float32))
    overall = trace_total(term, row_count, col_count, groups)
    trace_value = overall / math.sqrt(row_count * RB * width)
    return (totals.astype(jnp.bfloat16), trace_value)


def solution(mesh):
    return jax.shard_map(
        body,
        mesh=mesh,
        in_specs=(
            P("row", "col", None, None, None, None),
            P("row", "col", None, None),
            P("row", "col", None, None),
            P("row", "col", None),
        ),
        out_specs=(P("row", "col"), P()),
        check_vma=False,
    )
```

```python
import functools
import math

import jax
import jax.numpy as jnp
from jax import lax
from jax.experimental import pallas as pl
from jax.experimental.pallas import tpu as pltpu
from jax.sharding import PartitionSpec as P

RB = 5
STEPS = 4
MESH = pl.DeviceIdType.MESH


def densify(pieces, places, nrows, ncols):
    width = pieces.shape[-1]
    count = pieces.shape[0]
    onehot = (places[None, :] == jnp.arange(nrows * ncols, dtype=jnp.int32)[:, None]).astype(
        pieces.dtype
    )
    dense = jnp.dot(
        onehot, pieces.reshape(count, width * width), preferred_element_type=jnp.float32
    )
    dense = dense.reshape(nrows, ncols, width, width).transpose(0, 2, 1, 3)
    return dense.reshape(nrows * width, ncols * width).astype(pieces.dtype)


def exchange_kernel(row_count, col_count, groups,
                    blocks_ref, meta_ref, recv_l, recv_r, recv_ml, recv_mr, send_sem, recv_sem):
    r = lax.axis_index("row")
    c = lax.axis_index("col")
    a = r // groups
    b = r % groups

    def l_self(s):
        return (a + s) % col_count == 0

    def r_self(s):
        return (c + s) % col_count == 0

    def l_at(shift):
        return (r, (c + shift + 4 * col_count) % col_count)

    def r_at(shift):
        return ((r + shift + 4 * row_count) % row_count, c)

    left_plan, right_plan = {}, {}
    left_plan[1] = (l_self(1), l_at(-(a + 1)), l_at(a + 1))
    right_plan[1] = (r_self(1), r_at(-groups * (c + 1)), r_at(groups * (c + 1)))
    for s in (0, 2, 3):
        left_plan[s] = (l_self(s), l_at(1 - s), l_at(s - 1))
        right_plan[s] = (r_self(s), r_at(groups * (1 - s)), r_at(groups * (s - 1)))

    barrier = pltpu.get_barrier_semaphore()
    peers = 0
    for plan in (left_plan, right_plan):
        for s in range(STEPS):
            is_self, dst, src = plan[s]

            @pl.when(jnp.logical_not(is_self))
            def _(dst=dst, src=src):
                pl.semaphore_signal(barrier, 1, device_id=dst, device_id_type=MESH)
                pl.semaphore_signal(barrier, 1, device_id=src, device_id_type=MESH)

            peers = peers + jnp.where(is_self, 0, 2)
    pl.semaphore_wait(barrier, peers)

    sides = (
        (left_plan, blocks_ref.at[b], recv_l, 0),
        (left_plan, meta_ref, recv_ml, 1),
        (right_plan, blocks_ref, recv_r, 2),
        (right_plan, meta_ref, recv_mr, 3),
    )

    def transfer(plan, s, source, recv, j):
        is_self, dst, _ = plan[s]
        k = 4 * s + j
        local = pltpu.make_async_copy(source, recv.at[s], recv_sem.at[k])
        remote = pltpu.make_async_remote_copy(
            source, recv.at[s], send_sem.at[k], recv_sem.at[k],
            device_id=dst, device_id_type=MESH,
        )
        return is_self, local, remote

    def start(job, forward):
        is_self, local, remote = job

        if not forward:
            @pl.when(is_self)
            def _():
                local.start()

        @pl.when(jnp.logical_not(is_self))
        def _():
            remote.start()

    def finish_recv(job):
        is_self, local, remote = job

        @pl.when(is_self)
        def _():
            local.wait()

        @pl.when(jnp.logical_not(is_self))
        def _():
            remote.wait_recv()

    def finish_send(job):
        is_self, local, remote = job

        @pl.when(jnp.logical_not(is_self))
        def _():
            remote.wait_send()

    firsts = [transfer(plan, 1, source, recv, j) for plan, source, recv, j in sides]
    for job in firsts:
        start(job, False)
    forwards = []
    for plan, source, recv, j in sides:
        for s in (0, 2, 3):
            forwards.append(transfer(plan, s, recv.at[1], recv, j))
    for (plan, source, recv, j), first in zip(sides, firsts):
        finish_recv(first)
        for s in (0, 2, 3):
            is_self, local, remote = transfer(plan, s, source, recv, j)

            @pl.when(is_self)
            def _(local=local):
                local.start()
    for job in forwards:
        start(job, True)
    for job in forwards:
        finish_recv(job)
    for job in firsts + forwards:
        finish_send(job)


def exchange(blocks, meta, row_count, col_count):
    groups, slots, width = blocks.shape[0], blocks.shape[1], blocks.shape[2]
    vmem = pl.BlockSpec(memory_space=pltpu.VMEM)
    return pl.pallas_call(
        functools.partial(exchange_kernel, row_count, col_count, groups),
        out_shape=(
            jax.ShapeDtypeStruct((STEPS, slots, width, width), blocks.dtype),
            jax.ShapeDtypeStruct((STEPS, groups, slots, width, width), blocks.dtype),
            jax.ShapeDtypeStruct((STEPS,) + meta.shape, meta.dtype),
            jax.ShapeDtypeStruct((STEPS,) + meta.shape, meta.dtype),
        ),
        in_specs=[vmem, vmem],
        out_specs=(vmem, vmem, vmem, vmem),
        scratch_shapes=[
            pltpu.SemaphoreType.DMA((4 * STEPS,)),
            pltpu.SemaphoreType.DMA((4 * STEPS,)),
        ],
        compiler_params=pltpu.CompilerParams(collective_id=0, has_side_effects=True),
    )(blocks, meta)


def trace_kernel(row_count, col_count, groups,
                 term_ref, out_ref, row_buf, col_buf, send_sem, recv_sem, col_send, col_recv):
    r = lax.axis_index("row")
    c = lax.axis_index("col")
    diagonal = c == r // groups
    barrier = pltpu.get_barrier_semaphore()

    @pl.when(diagonal)
    def _():
        for cc in range(col_count):
            @pl.when(cc != c)
            def _(cc=cc):
                pl.semaphore_signal(barrier, 1, device_id=(r, cc), device_id_type=MESH)

    @pl.when(jnp.logical_not(diagonal))
    def _():
        pl.semaphore_signal(barrier, 1, device_id=(r, r // groups), device_id_type=MESH)

    for rr in range(row_count):
        @pl.when(rr != r)
        def _(rr=rr):
            pl.semaphore_signal(barrier, 1, device_id=(rr, c), device_id_type=MESH)

    pl.semaphore_wait(barrier, (row_count - 1) + jnp.where(diagonal, col_count - 1, 1))

    row_copies = []
    for cc in range(col_count):
        row_copies.append(pltpu.make_async_remote_copy(
            term_ref, row_buf, send_sem.at[cc], recv_sem.at[0],
            device_id=(r, cc), device_id_type=MESH,
        ))

    @pl.when(diagonal)
    def _():
        for cc in range(col_count):
            @pl.when(cc != c)
            def _(cc=cc):
                row_copies[cc].start()

    @pl.when(jnp.logical_not(diagonal))
    def _():
        row_copies[0].wait_recv()

    def col_copy(source, rr):
        return pltpu.make_async_remote_copy(
            source, col_buf.at[r], col_send.at[rr], col_recv.at[r],
            device_id=(rr, c), device_id_type=MESH,
        )

    for source, chosen in ((term_ref, diagonal), (row_buf, jnp.logical_not(diagonal))):
        @pl.when(chosen)
        def _(source=source):
            for rr in range(row_count):
                @pl.when(rr != r)
                def _(rr=rr):
                    col_copy(source, rr).start()

    for rr in range(row_count):
        @pl.when(rr != r)
        def _(rr=rr):
            pltpu.make_async_remote_copy(
                term_ref, col_buf.at[rr], col_send.at[rr], col_recv.at[rr],
                device_id=(rr, c), device_id_type=MESH,
            ).wait_recv()

    for source, chosen in ((term_ref, diagonal), (row_buf, jnp.logical_not(diagonal))):
        @pl.when(chosen)
        def _(source=source):
            for rr in range(row_count):
                @pl.when(rr != r)
                def _(rr=rr):
                    col_copy(source, rr).wait_send()
            col_buf[r] = source[...]

    @pl.when(diagonal)
    def _():
        for cc in range(col_count):
            @pl.when(cc != c)
            def _(cc=cc):
                row_copies[cc].wait_send()

    total = jnp.zeros(out_ref.shape, jnp.float32)
    for rr in range(row_count):
        total = total + col_buf[rr]
    out_ref[...] = total


def trace_total(term, row_count, col_count, groups):
    tile = jnp.broadcast_to(term, (8, 128))
    vmem = pl.BlockSpec(memory_space=pltpu.VMEM)
    out = pl.pallas_call(
        functools.partial(trace_kernel, row_count, col_count, groups),
        out_shape=jax.ShapeDtypeStruct((8, 128), jnp.float32),
        in_specs=[vmem],
        out_specs=vmem,
        scratch_shapes=[
            pltpu.VMEM((8, 128), jnp.float32),
            pltpu.VMEM((row_count, 8, 128), jnp.float32),
            pltpu.SemaphoreType.DMA((col_count,)),
            pltpu.SemaphoreType.DMA((1,)),
            pltpu.SemaphoreType.DMA((row_count,)),
            pltpu.SemaphoreType.DMA((row_count,)),
        ],
        compiler_params=pltpu.CompilerParams(collective_id=1, has_side_effects=True),
    )(tile)
    return out[0, 0]


def body(blocks, block_rows, block_cols, counts):
    groups = blocks.shape[2]
    slot_count = blocks.shape[3]
    width = blocks.shape[4]
    row_count = lax.axis_size("row")
    col_count = lax.axis_size("col")
    row_place = lax.axis_index("row")
    col_place = lax.axis_index("col")
    lower = row_place % groups
    filled = counts[0, 0]
    live = jnp.arange(slot_count, dtype=jnp.int32)[None, :] < filled[:, None]
    left_places_all = jnp.where(live, block_rows[0, 0] * RB + block_cols[0, 0], -1)
    offsets = (jnp.arange(groups, dtype=jnp.int32) * RB)[:, None]
    right_places = jnp.where(
        live, block_rows[0, 0] * (groups * RB) + block_cols[0, 0] + offsets, -1
    ).reshape(-1)
    left_places = lax.dynamic_index_in_dim(left_places_all, lower, 0, keepdims=False)
    meta = jnp.zeros((8, 128), jnp.int32)
    meta = meta.at[0, :slot_count].set(left_places)
    meta = meta.at[1, : groups * slot_count].set(right_places)
    recv_l, recv_r, recv_ml, recv_mr = exchange(blocks[0, 0], meta, row_count, col_count)
    totals = jnp.zeros((RB * width, groups * RB * width), jnp.float32)
    for step in range(STEPS):
        rp = recv_r[step].reshape(groups * slot_count, width, width)
        right_dense = densify(rp, recv_mr[step, 1, : groups * slot_count], RB, groups * RB)
        left_dense = densify(recv_l[step], recv_ml[step, 0, :slot_count], RB, RB)
        totals = totals + jnp.dot(left_dense, right_dense, preferred_element_type=jnp.float32)
    shift_amount = row_place - groups * col_place
    valid = (shift_amount >= 0) & (shift_amount < groups)
    start = jnp.clip(shift_amount, 0, groups - 1) * RB * width
    window = lax.dynamic_slice_in_dim(totals, start, RB * width, 1)
    term = jnp.where(valid, jnp.trace(window), jnp.zeros((), jnp.float32))
    overall = trace_total(term, row_count, col_count, groups)
    trace_value = overall / math.sqrt(row_count * RB * width)
    return (totals.astype(jnp.bfloat16), trace_value)


def solution(mesh):
    return jax.shard_map(
        body,
        mesh=mesh,
        in_specs=(
            P("row", "col", None, None, None, None),
            P("row", "col", None, None),
            P("row", "col", None, None),
            P("row", "col", None),
        ),
        out_specs=(P("row", "col"), P()),
        check_vma=False,
    )
```

```python
import functools
import math

import jax
import jax.numpy as jnp
from jax import lax
from jax.experimental import pallas as pl
from jax.experimental.pallas import tpu as pltpu
from jax.sharding import PartitionSpec as P

RB = 5
STEPS = 4
MESH = pl.DeviceIdType.MESH


def densify(pieces, places, nrows, ncols):
    width = pieces.shape[-1]
    count = pieces.shape[0]
    onehot = (places[None, :] == jnp.arange(nrows * ncols, dtype=jnp.int32)[:, None]).astype(
        pieces.dtype
    )
    dense = jnp.dot(
        onehot, pieces.reshape(count, width * width), preferred_element_type=jnp.float32
    )
    dense = dense.reshape(nrows, ncols, width, width).transpose(0, 2, 1, 3)
    return dense.reshape(nrows * width, ncols * width).astype(pieces.dtype)


def exchange_kernel(row_count, col_count, groups,
                    blocks_ref, meta_ref, recv_l, recv_r, recv_ml, recv_mr, send_sem, recv_sem):
    r = lax.axis_index("row")
    c = lax.axis_index("col")
    a = r // groups
    b = r % groups

    def l_self(s):
        return (a + s) % col_count == 0

    def r_self(s):
        return (c + s) % col_count == 0

    def l_at(shift):
        return (r, (c + shift + 4 * col_count) % col_count)

    def r_at(shift):
        return ((r + shift + 4 * row_count) % row_count, c)

    left_plan, right_plan = {}, {}
    left_plan[1] = (l_self(1), l_at(-(a + 1)), l_at(a + 1))
    right_plan[1] = (r_self(1), r_at(-groups * (c + 1)), r_at(groups * (c + 1)))
    for s in (0, 2, 3):
        left_plan[s] = (l_self(s), l_at(1 - s), l_at(s - 1))
        right_plan[s] = (r_self(s), r_at(groups * (1 - s)), r_at(groups * (s - 1)))

    barrier = pltpu.get_barrier_semaphore()
    peers = 0
    for plan in (left_plan, right_plan):
        for s in range(STEPS):
            is_self, dst, src = plan[s]

            @pl.when(jnp.logical_not(is_self))
            def _(dst=dst, src=src):
                pl.semaphore_signal(barrier, 1, device_id=dst, device_id_type=MESH)
                pl.semaphore_signal(barrier, 1, device_id=src, device_id_type=MESH)

            peers = peers + jnp.where(is_self, 0, 2)
    pl.semaphore_wait(barrier, peers)

    sides = (
        (left_plan, blocks_ref.at[b], recv_l, 0),
        (left_plan, meta_ref, recv_ml, 1),
        (right_plan, blocks_ref, recv_r, 2),
        (right_plan, meta_ref, recv_mr, 3),
    )

    def transfer(plan, s, source, recv, j):
        is_self, dst, _ = plan[s]
        k = 4 * s + j
        local = pltpu.make_async_copy(source, recv.at[s], recv_sem.at[k])
        remote = pltpu.make_async_remote_copy(
            source, recv.at[s], send_sem.at[k], recv_sem.at[k],
            device_id=dst, device_id_type=MESH,
        )
        return is_self, local, remote

    def start(job, forward):
        is_self, local, remote = job

        if not forward:
            @pl.when(is_self)
            def _():
                local.start()

        @pl.when(jnp.logical_not(is_self))
        def _():
            remote.start()

    def finish_recv(job):
        is_self, local, remote = job

        @pl.when(is_self)
        def _():
            local.wait()

        @pl.when(jnp.logical_not(is_self))
        def _():
            remote.wait_recv()

    def finish_send(job):
        is_self, local, remote = job

        @pl.when(jnp.logical_not(is_self))
        def _():
            remote.wait_send()

    firsts = [transfer(plan, 1, source, recv, j) for plan, source, recv, j in sides]
    for job in firsts:
        start(job, False)
    forwards = []
    for plan, source, recv, j in sides:
        for s in (0, 2, 3):
            forwards.append(transfer(plan, s, recv.at[1], recv, j))
    for (plan, source, recv, j), first in zip(sides, firsts):
        finish_recv(first)
        for s in (0, 2, 3):
            is_self, local, remote = transfer(plan, s, source, recv, j)

            @pl.when(is_self)
            def _(local=local):
                local.start()
    for job in forwards:
        start(job, True)
    for job in forwards:
        finish_recv(job)
    for job in firsts + forwards:
        finish_send(job)


def exchange(blocks, meta, row_count, col_count):
    groups, slots, width = blocks.shape[0], blocks.shape[1], blocks.shape[2]
    vmem = pl.BlockSpec(memory_space=pltpu.VMEM)
    return pl.pallas_call(
        functools.partial(exchange_kernel, row_count, col_count, groups),
        out_shape=(
            jax.ShapeDtypeStruct((STEPS, slots, width, width), blocks.dtype),
            jax.ShapeDtypeStruct((STEPS, groups, slots, width, width), blocks.dtype),
            jax.ShapeDtypeStruct((STEPS,) + meta.shape, meta.dtype),
            jax.ShapeDtypeStruct((STEPS,) + meta.shape, meta.dtype),
        ),
        in_specs=[vmem, vmem],
        out_specs=(vmem, vmem, vmem, vmem),
        scratch_shapes=[
            pltpu.SemaphoreType.DMA((4 * STEPS,)),
            pltpu.SemaphoreType.DMA((4 * STEPS,)),
        ],
        compiler_params=pltpu.CompilerParams(collective_id=0, has_side_effects=True),
    )(blocks, meta)


def trace_kernel(row_count, col_count, groups,
                 term_ref, out_ref, row_buf, col_buf, send_sem, recv_sem, col_send, col_recv):
    r = lax.axis_index("row")
    c = lax.axis_index("col")
    diagonal = c == r // groups
    rounds = (row_count - 1).bit_length()
    barrier = pltpu.get_barrier_semaphore()

    @pl.when(diagonal)
    def _():
        for cc in range(col_count):
            @pl.when(cc != c)
            def _(cc=cc):
                pl.semaphore_signal(barrier, 1, device_id=(r, cc), device_id_type=MESH)

    @pl.when(jnp.logical_not(diagonal))
    def _():
        pl.semaphore_signal(barrier, 1, device_id=(r, r // groups), device_id_type=MESH)

    for k in range(rounds):
        pl.semaphore_signal(barrier, 1, device_id=(r ^ (1 << k), c), device_id_type=MESH)

    pl.semaphore_wait(barrier, rounds + jnp.where(diagonal, col_count - 1, 1))

    row_copies = []
    for cc in range(col_count):
        row_copies.append(pltpu.make_async_remote_copy(
            term_ref, row_buf, send_sem.at[cc], recv_sem.at[0],
            device_id=(r, cc), device_id_type=MESH,
        ))

    @pl.when(diagonal)
    def _():
        for cc in range(col_count):
            @pl.when(cc != c)
            def _(cc=cc):
                row_copies[cc].start()

    @pl.when(jnp.logical_not(diagonal))
    def _():
        row_copies[0].wait_recv()

    partner = r ^ 1
    for source, chosen in ((term_ref, diagonal), (row_buf, jnp.logical_not(diagonal))):
        @pl.when(chosen)
        def _(source=source):
            own = pltpu.make_async_copy(source, col_buf.at[r], recv_sem.at[1])
            first = pltpu.make_async_remote_copy(
                source, col_buf.at[r], col_send.at[0], col_recv.at[0],
                device_id=(partner, c), device_id_type=MESH,
            )
            own.start()
            first.start()
            own.wait()
            first.wait_send()

    pltpu.make_async_remote_copy(
        term_ref, col_buf.at[partner], col_send.at[0], col_recv.at[0],
        device_id=(partner, c), device_id_type=MESH,
    ).wait_recv()

    for k in range(1, rounds):
        size = 1 << k
        partner = r ^ size
        mine = pl.ds(pl.multiple_of(r - r % size, size), size)
        theirs = pl.ds(pl.multiple_of(partner - partner % size, size), size)
        step = pltpu.make_async_remote_copy(
            col_buf.at[mine], col_buf.at[mine], col_send.at[k], col_recv.at[k],
            device_id=(partner, c), device_id_type=MESH,
        )
        step.start()
        pltpu.make_async_remote_copy(
            col_buf.at[theirs], col_buf.at[theirs], col_send.at[k], col_recv.at[k],
            device_id=(partner, c), device_id_type=MESH,
        ).wait_recv()
        step.wait_send()

    @pl.when(diagonal)
    def _():
        for cc in range(col_count):
            @pl.when(cc != c)
            def _(cc=cc):
                row_copies[cc].wait_send()

    total = jnp.zeros(out_ref.shape, jnp.float32)
    for rr in range(row_count):
        total = total + col_buf[rr]
    out_ref[...] = total


def trace_total(term, row_count, col_count, groups):
    tile = jnp.broadcast_to(term, (8, 128))
    vmem = pl.BlockSpec(memory_space=pltpu.VMEM)
    out = pl.pallas_call(
        functools.partial(trace_kernel, row_count, col_count, groups),
        out_shape=jax.ShapeDtypeStruct((8, 128), jnp.float32),
        in_specs=[vmem],
        out_specs=vmem,
        scratch_shapes=[
            pltpu.VMEM((8, 128), jnp.float32),
            pltpu.VMEM((row_count, 8, 128), jnp.float32),
            pltpu.SemaphoreType.DMA((col_count,)),
            pltpu.SemaphoreType.DMA((2,)),
            pltpu.SemaphoreType.DMA((row_count,)),
            pltpu.SemaphoreType.DMA((row_count,)),
        ],
        compiler_params=pltpu.CompilerParams(collective_id=1, has_side_effects=True),
    )(tile)
    return out[0, 0]


def body(blocks, block_rows, block_cols, counts):
    groups = blocks.shape[2]
    slot_count = blocks.shape[3]
    width = blocks.shape[4]
    row_count = lax.axis_size("row")
    col_count = lax.axis_size("col")
    row_place = lax.axis_index("row")
    col_place = lax.axis_index("col")
    lower = row_place % groups
    filled = counts[0, 0]
    live = jnp.arange(slot_count, dtype=jnp.int32)[None, :] < filled[:, None]
    left_places_all = jnp.where(live, block_rows[0, 0] * RB + block_cols[0, 0], -1)
    offsets = (jnp.arange(groups, dtype=jnp.int32) * RB)[:, None]
    right_places = jnp.where(
        live, block_rows[0, 0] * (groups * RB) + block_cols[0, 0] + offsets, -1
    ).reshape(-1)
    left_places = lax.dynamic_index_in_dim(left_places_all, lower, 0, keepdims=False)
    meta = jnp.zeros((8, 128), jnp.int32)
    meta = meta.at[0, :slot_count].set(left_places)
    meta = meta.at[1, : groups * slot_count].set(right_places)
    recv_l, recv_r, recv_ml, recv_mr = exchange(blocks[0, 0], meta, row_count, col_count)
    totals = jnp.zeros((RB * width, groups * RB * width), jnp.float32)
    for step in range(STEPS):
        rp = recv_r[step].reshape(groups * slot_count, width, width)
        right_dense = densify(rp, recv_mr[step, 1, : groups * slot_count], RB, groups * RB)
        left_dense = densify(recv_l[step], recv_ml[step, 0, :slot_count], RB, RB)
        totals = totals + jnp.dot(left_dense, right_dense, preferred_element_type=jnp.float32)
    shift_amount = row_place - groups * col_place
    valid = (shift_amount >= 0) & (shift_amount < groups)
    start = jnp.clip(shift_amount, 0, groups - 1) * RB * width
    window = lax.dynamic_slice_in_dim(totals, start, RB * width, 1)
    term = jnp.where(valid, jnp.trace(window), jnp.zeros((), jnp.float32))
    overall = trace_total(term, row_count, col_count, groups)
    trace_value = overall / math.sqrt(row_count * RB * width)
    return (totals.astype(jnp.bfloat16), trace_value)


def solution(mesh):
    return jax.shard_map(
        body,
        mesh=mesh,
        in_specs=(
            P("row", "col", None, None, None, None),
            P("row", "col", None, None),
            P("row", "col", None, None),
            P("row", "col", None),
        ),
        out_specs=(P("row", "col"), P()),
        check_vma=False,
    )
```

```python
import functools
import math

import jax
import jax.numpy as jnp
from jax import lax
from jax.experimental import pallas as pl
from jax.experimental.pallas import tpu as pltpu
from jax.sharding import PartitionSpec as P

RB = 5
STEPS = 4
MESH = pl.DeviceIdType.MESH


def densify(pieces, places, nrows, ncols):
    width = pieces.shape[-1]
    count = pieces.shape[0]
    onehot = (places[None, :] == jnp.arange(nrows * ncols, dtype=jnp.int32)[:, None]).astype(
        pieces.dtype
    )
    dense = jnp.dot(
        onehot, pieces.reshape(count, width * width), preferred_element_type=jnp.float32
    )
    dense = dense.reshape(nrows, ncols, width, width).transpose(0, 2, 1, 3)
    return dense.reshape(nrows * width, ncols * width).astype(pieces.dtype)


def exchange_kernel(row_count, col_count, groups,
                    blocks_ref, meta_ref, recv_l, recv_r, recv_ml, recv_mr, send_sem, recv_sem):
    r = lax.axis_index("row")
    c = lax.axis_index("col")
    a = r // groups
    b = r % groups

    def l_self(s):
        return (a + s) % col_count == 0

    def r_self(s):
        return (c + s) % col_count == 0

    def l_at(shift):
        return (r, (c + shift + 4 * col_count) % col_count)

    def r_at(shift):
        return ((r + shift + 4 * row_count) % row_count, c)

    left_plan, right_plan = {}, {}
    left_plan[1] = (l_self(1), l_at(-(a + 1)), l_at(a + 1))
    right_plan[1] = (r_self(1), r_at(-groups * (c + 1)), r_at(groups * (c + 1)))
    for s in (0, 2, 3):
        left_plan[s] = (l_self(s), l_at(1 - s), l_at(s - 1))
        right_plan[s] = (r_self(s), r_at(groups * (1 - s)), r_at(groups * (s - 1)))

    barrier = pltpu.get_barrier_semaphore()
    peers = 0
    for plan in (left_plan, right_plan):
        for s in range(STEPS):
            is_self, dst, src = plan[s]

            @pl.when(jnp.logical_not(is_self))
            def _(dst=dst, src=src):
                pl.semaphore_signal(barrier, 1, device_id=dst, device_id_type=MESH)
                pl.semaphore_signal(barrier, 1, device_id=src, device_id_type=MESH)

            peers = peers + jnp.where(is_self, 0, 2)
    pl.semaphore_wait(barrier, peers)

    sides = [
        (left_plan, meta_ref, lambda s: recv_ml.at[s]),
        (right_plan, meta_ref, lambda s: recv_mr.at[s]),
        (left_plan, blocks_ref.at[b], lambda s: recv_l.at[s]),
    ]
    for g in range(groups):
        sides.append((right_plan, blocks_ref.at[g], lambda s, g=g: recv_r.at[s, g]))
    kinds = len(sides)

    def transfer(plan, s, source, target, j):
        is_self, dst, _ = plan[s]
        k = kinds * s + j
        local = pltpu.make_async_copy(source, target, recv_sem.at[k])
        remote = pltpu.make_async_remote_copy(
            source, target, send_sem.at[k], recv_sem.at[k],
            device_id=dst, device_id_type=MESH,
        )
        return is_self, local, remote

    def finish_recv(job):
        is_self, local, remote = job

        @pl.when(is_self)
        def _():
            local.wait()

        @pl.when(jnp.logical_not(is_self))
        def _():
            remote.wait_recv()

    firsts = []
    for j, (plan, source, target) in enumerate(sides):
        job = transfer(plan, 1, source, target(1), j)
        firsts.append(job)
        is_self, local, remote = job

        @pl.when(is_self)
        def _(local=local):
            local.start()

        @pl.when(jnp.logical_not(is_self))
        def _(remote=remote):
            remote.start()

    for j, (plan, source, target) in enumerate(sides):
        for s in (0, 2, 3):
            is_self, local, remote = transfer(plan, s, source, target(s), j)

            @pl.when(is_self)
            def _(local=local):
                local.start()

    forwards = []
    for j, (plan, source, target) in enumerate(sides):
        finish_recv(firsts[j])
        for s in (0, 2, 3):
            job = transfer(plan, s, target(1), target(s), j)
            forwards.append(job)
            is_self, local, remote = job

            @pl.when(jnp.logical_not(is_self))
            def _(remote=remote):
                remote.start()

    for job in forwards:
        finish_recv(job)
    for is_self, local, remote in firsts + forwards:
        @pl.when(jnp.logical_not(is_self))
        def _(remote=remote):
            remote.wait_send()


def exchange(blocks, meta, row_count, col_count):
    groups, slots, width = blocks.shape[0], blocks.shape[1], blocks.shape[2]
    vmem = pl.BlockSpec(memory_space=pltpu.VMEM)
    return pl.pallas_call(
        functools.partial(exchange_kernel, row_count, col_count, groups),
        out_shape=(
            jax.ShapeDtypeStruct((STEPS, slots, width, width), blocks.dtype),
            jax.ShapeDtypeStruct((STEPS, groups, slots, width, width), blocks.dtype),
            jax.ShapeDtypeStruct((STEPS,) + meta.shape, meta.dtype),
            jax.ShapeDtypeStruct((STEPS,) + meta.shape, meta.dtype),
        ),
        in_specs=[vmem, vmem],
        out_specs=(vmem, vmem, vmem, vmem),
        scratch_shapes=[
            pltpu.SemaphoreType.DMA(((3 + groups) * STEPS,)),
            pltpu.SemaphoreType.DMA(((3 + groups) * STEPS,)),
        ],
        compiler_params=pltpu.CompilerParams(collective_id=0, has_side_effects=True),
    )(blocks, meta)


def trace_kernel(row_count, col_count, groups,
                 term_ref, out_ref, row_buf, col_buf, send_sem, recv_sem, col_send, col_recv):
    r = lax.axis_index("row")
    c = lax.axis_index("col")
    diagonal = c == r // groups
    barrier = pltpu.get_barrier_semaphore()

    @pl.when(diagonal)
    def _():
        for cc in range(col_count):
            @pl.when(cc != c)
            def _(cc=cc):
                pl.semaphore_signal(barrier, 1, device_id=(r, cc), device_id_type=MESH)

    @pl.when(jnp.logical_not(diagonal))
    def _():
        pl.semaphore_signal(barrier, 1, device_id=(r, r // groups), device_id_type=MESH)

    for rr in range(row_count):
        @pl.when(rr != r)
        def _(rr=rr):
            pl.semaphore_signal(barrier, 1, device_id=(rr, c), device_id_type=MESH)

    pl.semaphore_wait(barrier, (row_count - 1) + jnp.where(diagonal, col_count - 1, 1))

    row_copies = []
    for cc in range(col_count):
        row_copies.append(pltpu.make_async_remote_copy(
            term_ref, row_buf, send_sem.at[cc], recv_sem.at[0],
            device_id=(r, cc), device_id_type=MESH,
        ))

    @pl.when(diagonal)
    def _():
        for cc in range(col_count):
            @pl.when(cc != c)
            def _(cc=cc):
                row_copies[cc].start()

    @pl.when(jnp.logical_not(diagonal))
    def _():
        row_copies[0].wait_recv()

    def col_copy(source, rr):
        return pltpu.make_async_remote_copy(
            source, col_buf.at[r], col_send.at[rr], col_recv.at[r],
            device_id=(rr, c), device_id_type=MESH,
        )

    for source, chosen in ((term_ref, diagonal), (row_buf, jnp.logical_not(diagonal))):
        @pl.when(chosen)
        def _(source=source):
            for rr in range(row_count):
                @pl.when(rr != r)
                def _(rr=rr):
                    col_copy(source, rr).start()

    for rr in range(row_count):
        @pl.when(rr != r)
        def _(rr=rr):
            pltpu.make_async_remote_copy(
                term_ref, col_buf.at[rr], col_send.at[rr], col_recv.at[rr],
                device_id=(rr, c), device_id_type=MESH,
            ).wait_recv()

    for source, chosen in ((term_ref, diagonal), (row_buf, jnp.logical_not(diagonal))):
        @pl.when(chosen)
        def _(source=source):
            for rr in range(row_count):
                @pl.when(rr != r)
                def _(rr=rr):
                    col_copy(source, rr).wait_send()
            col_buf[r] = source[...]

    @pl.when(diagonal)
    def _():
        for cc in range(col_count):
            @pl.when(cc != c)
            def _(cc=cc):
                row_copies[cc].wait_send()

    total = jnp.zeros(out_ref.shape, jnp.float32)
    for rr in range(row_count):
        total = total + col_buf[rr]
    out_ref[...] = total


def trace_total(term, row_count, col_count, groups):
    tile = jnp.broadcast_to(term, (8, 128))
    vmem = pl.BlockSpec(memory_space=pltpu.VMEM)
    out = pl.pallas_call(
        functools.partial(trace_kernel, row_count, col_count, groups),
        out_shape=jax.ShapeDtypeStruct((8, 128), jnp.float32),
        in_specs=[vmem],
        out_specs=vmem,
        scratch_shapes=[
            pltpu.VMEM((8, 128), jnp.float32),
            pltpu.VMEM((row_count, 8, 128), jnp.float32),
            pltpu.SemaphoreType.DMA((col_count,)),
            pltpu.SemaphoreType.DMA((1,)),
            pltpu.SemaphoreType.DMA((row_count,)),
            pltpu.SemaphoreType.DMA((row_count,)),
        ],
        compiler_params=pltpu.CompilerParams(collective_id=1, has_side_effects=True),
    )(tile)
    return out[0, 0]


def body(blocks, block_rows, block_cols, counts):
    groups = blocks.shape[2]
    slot_count = blocks.shape[3]
    width = blocks.shape[4]
    row_count = lax.axis_size("row")
    col_count = lax.axis_size("col")
    row_place = lax.axis_index("row")
    col_place = lax.axis_index("col")
    lower = row_place % groups
    filled = counts[0, 0]
    live = jnp.arange(slot_count, dtype=jnp.int32)[None, :] < filled[:, None]
    left_places_all = jnp.where(live, block_rows[0, 0] * RB + block_cols[0, 0], -1)
    offsets = (jnp.arange(groups, dtype=jnp.int32) * RB)[:, None]
    right_places = jnp.where(
        live, block_rows[0, 0] * (groups * RB) + block_cols[0, 0] + offsets, -1
    ).reshape(-1)
    left_places = lax.dynamic_index_in_dim(left_places_all, lower, 0, keepdims=False)
    meta = jnp.zeros((8, 128), jnp.int32)
    meta = meta.at[0, :slot_count].set(left_places)
    meta = meta.at[1, : groups * slot_count].set(right_places)
    recv_l, recv_r, recv_ml, recv_mr = exchange(blocks[0, 0], meta, row_count, col_count)
    totals = jnp.zeros((RB * width, groups * RB * width), jnp.float32)
    for step in range(STEPS):
        rp = recv_r[step].reshape(groups * slot_count, width, width)
        right_dense = densify(rp, recv_mr[step, 1, : groups * slot_count], RB, groups * RB)
        left_dense = densify(recv_l[step], recv_ml[step, 0, :slot_count], RB, RB)
        totals = totals + jnp.dot(left_dense, right_dense, preferred_element_type=jnp.float32)
    shift_amount = row_place - groups * col_place
    valid = (shift_amount >= 0) & (shift_amount < groups)
    start = jnp.clip(shift_amount, 0, groups - 1) * RB * width
    window = lax.dynamic_slice_in_dim(totals, start, RB * width, 1)
    term = jnp.where(valid, jnp.trace(window), jnp.zeros((), jnp.float32))
    overall = trace_total(term, row_count, col_count, groups)
    trace_value = overall / math.sqrt(row_count * RB * width)
    return (totals.astype(jnp.bfloat16), trace_value)


def solution(mesh):
    return jax.shard_map(
        body,
        mesh=mesh,
        in_specs=(
            P("row", "col", None, None, None, None),
            P("row", "col", None, None),
            P("row", "col", None, None),
            P("row", "col", None),
        ),
        out_specs=(P("row", "col"), P()),
        check_vma=False,
    )
```

```python
import functools
import math

import jax
import jax.numpy as jnp
from jax import lax
from jax.experimental import pallas as pl
from jax.experimental.pallas import tpu as pltpu
from jax.sharding import PartitionSpec as P

RB = 5
STEPS = 4
MESH = pl.DeviceIdType.MESH


def densify(pieces, places, nrows, ncols):
    width = pieces.shape[-1]
    count = pieces.shape[0]
    onehot = (places[None, :] == jnp.arange(nrows * ncols, dtype=jnp.int32)[:, None]).astype(
        pieces.dtype
    )
    dense = jnp.dot(
        onehot, pieces.reshape(count, width * width), preferred_element_type=jnp.float32
    )
    dense = dense.reshape(nrows, ncols, width, width).transpose(0, 2, 1, 3)
    return dense.reshape(nrows * width, ncols * width).astype(pieces.dtype)


def exchange_kernel(row_count, col_count, groups,
                    blocks_ref, meta_ref, recv_l, recv_r, recv_ml, recv_mr, total_ref,
                    send_sem, recv_sem, term_buf, row_buf, col_buf, t_send, t_recv, c_send, c_recv):
    r = lax.axis_index("row")
    c = lax.axis_index("col")
    a = r // groups
    b = r % groups

    def l_self(s):
        return (a + s) % col_count == 0

    def r_self(s):
        return (c + s) % col_count == 0

    def l_at(shift):
        return (r, (c + shift + 4 * col_count) % col_count)

    def r_at(shift):
        return ((r + shift + 4 * row_count) % row_count, c)

    left_plan, right_plan = {}, {}
    left_plan[1] = (l_self(1), l_at(-(a + 1)), l_at(a + 1))
    right_plan[1] = (r_self(1), r_at(-groups * (c + 1)), r_at(groups * (c + 1)))
    for s in (0, 2, 3):
        left_plan[s] = (l_self(s), l_at(1 - s), l_at(s - 1))
        right_plan[s] = (r_self(s), r_at(groups * (1 - s)), r_at(groups * (s - 1)))

    barrier = pltpu.get_barrier_semaphore()
    peers = 0
    for plan in (left_plan, right_plan):
        for s in range(STEPS):
            is_self, dst, src = plan[s]

            @pl.when(jnp.logical_not(is_self))
            def _(dst=dst, src=src):
                pl.semaphore_signal(barrier, 1, device_id=dst, device_id_type=MESH)
                pl.semaphore_signal(barrier, 1, device_id=src, device_id_type=MESH)

            peers = peers + jnp.where(is_self, 0, 2)
    diagonal = c == a
    slots = blocks_ref.shape[1]
    width = blocks_ref.shape[2]

    @pl.when(diagonal)
    def _():
        for cc in range(col_count):
            @pl.when(cc != c)
            def _(cc=cc):
                pl.semaphore_signal(barrier, 1, device_id=(r, cc), device_id_type=MESH)

    @pl.when(jnp.logical_not(diagonal))
    def _():
        pl.semaphore_signal(barrier, 1, device_id=(r, a), device_id_type=MESH)

    for rr in range(row_count):
        @pl.when(rr != r)
        def _(rr=rr):
            pl.semaphore_signal(barrier, 1, device_id=(rr, c), device_id_type=MESH)

    peers = peers + (row_count - 1) + jnp.where(diagonal, col_count - 1, 1)
    pl.semaphore_wait(barrier, peers)

    sides = [
        (left_plan, meta_ref, lambda s: recv_ml.at[s]),
        (right_plan, meta_ref, lambda s: recv_mr.at[s]),
        (left_plan, blocks_ref.at[b], lambda s: recv_l.at[s]),
    ]
    for g in range(groups):
        sides.append((right_plan, blocks_ref.at[g], lambda s, g=g: recv_r.at[s, g]))
    kinds = len(sides)

    def transfer(plan, s, source, target, j):
        is_self, dst, _ = plan[s]
        k = kinds * s + j
        local = pltpu.make_async_copy(source, target, recv_sem.at[k])
        remote = pltpu.make_async_remote_copy(
            source, target, send_sem.at[k], recv_sem.at[k],
            device_id=dst, device_id_type=MESH,
        )
        return is_self, local, remote

    def finish_recv(job):
        is_self, local, remote = job

        @pl.when(is_self)
        def _():
            local.wait()

        @pl.when(jnp.logical_not(is_self))
        def _():
            remote.wait_recv()

    firsts = []
    for j, (plan, source, target) in enumerate(sides):
        job = transfer(plan, 1, source, target(1), j)
        firsts.append(job)
        is_self, local, remote = job

        @pl.when(is_self)
        def _(local=local):
            local.start()

        @pl.when(jnp.logical_not(is_self))
        def _(remote=remote):
            remote.start()

    for j, (plan, source, target) in enumerate(sides):
        for s in (0, 2, 3):
            is_self, local, remote = transfer(plan, s, source, target(s), j)

            @pl.when(is_self)
            def _(local=local):
                local.start()

    forwards = []
    for j, (plan, source, target) in enumerate(sides):
        finish_recv(firsts[j])
        for s in (0, 2, 3):
            job = transfer(plan, s, target(1), target(s), j)
            forwards.append(job)
            is_self, local, remote = job

            @pl.when(jnp.logical_not(is_self))
            def _(remote=remote):
                remote.start()

    for job in forwards:
        finish_recv(job)
    for is_self, local, remote in firsts + forwards:
        @pl.when(jnp.logical_not(is_self))
        def _(remote=remote):
            remote.wait_send()

    @pl.when(diagonal)
    def _():
        rows_i = lax.broadcasted_iota(jnp.int32, (width, slots * width), 0)
        cols_i = lax.broadcasted_iota(jnp.int32, (width, slots * width), 1)
        on_diag = rows_i == cols_i % width
        acc = jnp.zeros((1, 1), jnp.float32)
        for s in range(STEPS):
            rm = recv_mr.at[s]
            lm = recv_ml.at[s]
            rrow = jnp.concatenate(
                [rm[pl.ds(16 + slots * b + u, 1), :] for u in range(slots)], axis=1)
            rcol = jnp.concatenate(
                [rm[pl.ds(32 + slots * b + u, 1), :] for u in range(slots)], axis=1)
            right = jnp.concatenate([recv_r[s, b, u] for u in range(slots)], axis=1)
            for t in range(slots):
                lrow = jnp.concatenate([lm[t:t + 1, :]] * slots, axis=1)
                lcol = jnp.concatenate([lm[8 + t:9 + t, :]] * slots, axis=1)
                meet = (lcol == rrow) & (lrow == rcol)
                prod = jnp.dot(recv_l[s, t], right, preferred_element_type=jnp.float32)
                picked = jnp.where(on_diag & meet, prod, 0.0)
                acc = acc + jnp.sum(picked, keepdims=True)
        term_buf[...] = jnp.broadcast_to(acc, term_buf.shape)

    row_copies = []
    for cc in range(col_count):
        row_copies.append(pltpu.make_async_remote_copy(
            term_buf, row_buf, t_send.at[cc], t_recv.at[0],
            device_id=(r, cc), device_id_type=MESH,
        ))

    @pl.when(diagonal)
    def _():
        for cc in range(col_count):
            @pl.when(cc != c)
            def _(cc=cc):
                row_copies[cc].start()

    @pl.when(jnp.logical_not(diagonal))
    def _():
        row_copies[0].wait_recv()

    def col_copy(source, rr):
        return pltpu.make_async_remote_copy(
            source, col_buf.at[r], c_send.at[rr], c_recv.at[r],
            device_id=(rr, c), device_id_type=MESH,
        )

    for source, chosen in ((term_buf, diagonal), (row_buf, jnp.logical_not(diagonal))):
        @pl.when(chosen)
        def _(source=source):
            for rr in range(row_count):
                @pl.when(rr != r)
                def _(rr=rr):
                    col_copy(source, rr).start()

    for rr in range(row_count):
        @pl.when(rr != r)
        def _(rr=rr):
            pltpu.make_async_remote_copy(
                term_buf, col_buf.at[rr], c_send.at[rr], c_recv.at[rr],
                device_id=(rr, c), device_id_type=MESH,
            ).wait_recv()

    for source, chosen in ((term_buf, diagonal), (row_buf, jnp.logical_not(diagonal))):
        @pl.when(chosen)
        def _(source=source):
            for rr in range(row_count):
                @pl.when(rr != r)
                def _(rr=rr):
                    col_copy(source, rr).wait_send()
            col_buf[r] = source[...]

    @pl.when(diagonal)
    def _():
        for cc in range(col_count):
            @pl.when(cc != c)
            def _(cc=cc):
                row_copies[cc].wait_send()

    total = jnp.zeros(total_ref.shape, jnp.float32)
    for rr in range(row_count):
        total = total + col_buf[rr]
    total_ref[...] = total


def exchange(blocks, meta, row_count, col_count):
    groups, slots, width = blocks.shape[0], blocks.shape[1], blocks.shape[2]
    vmem = pl.BlockSpec(memory_space=pltpu.VMEM)
    kinds = 3 + groups
    return pl.pallas_call(
        functools.partial(exchange_kernel, row_count, col_count, groups),
        out_shape=(
            jax.ShapeDtypeStruct((STEPS, slots, width, width), blocks.dtype),
            jax.ShapeDtypeStruct((STEPS, groups, slots, width, width), blocks.dtype),
            jax.ShapeDtypeStruct((STEPS,) + meta.shape, meta.dtype),
            jax.ShapeDtypeStruct((STEPS,) + meta.shape, meta.dtype),
            jax.ShapeDtypeStruct((8, 128), jnp.float32),
        ),
        in_specs=[vmem, vmem],
        out_specs=(vmem, vmem, vmem, vmem, vmem),
        scratch_shapes=[
            pltpu.SemaphoreType.DMA((kinds * STEPS,)),
            pltpu.SemaphoreType.DMA((kinds * STEPS,)),
            pltpu.VMEM((8, 128), jnp.float32),
            pltpu.VMEM((8, 128), jnp.float32),
            pltpu.VMEM((row_count, 8, 128), jnp.float32),
            pltpu.SemaphoreType.DMA((col_count,)),
            pltpu.SemaphoreType.DMA((1,)),
            pltpu.SemaphoreType.DMA((row_count,)),
            pltpu.SemaphoreType.DMA((row_count,)),
        ],
        compiler_params=pltpu.CompilerParams(collective_id=0, has_side_effects=True),
    )(blocks, meta)


def body(blocks, block_rows, block_cols, counts):
    groups = blocks.shape[2]
    slot_count = blocks.shape[3]
    width = blocks.shape[4]
    row_count = lax.axis_size("row")
    col_count = lax.axis_size("col")
    row_place = lax.axis_index("row")
    col_place = lax.axis_index("col")
    lower = row_place % groups
    filled = counts[0, 0]
    live = jnp.arange(slot_count, dtype=jnp.int32)[None, :] < filled[:, None]
    left_places_all = jnp.where(live, block_rows[0, 0] * RB + block_cols[0, 0], -1)
    offsets = (jnp.arange(groups, dtype=jnp.int32) * RB)[:, None]
    right_places = jnp.where(
        live, block_rows[0, 0] * (groups * RB) + block_cols[0, 0] + offsets, -1
    ).reshape(-1)
    left_places = lax.dynamic_index_in_dim(left_places_all, lower, 0, keepdims=False)
    brows = block_rows[0, 0]
    bcols = block_cols[0, 0]
    left_live = lax.dynamic_index_in_dim(live, lower, 0, keepdims=False)
    lrow = jnp.where(left_live, lax.dynamic_index_in_dim(brows, lower, 0, keepdims=False), -100)
    lcol = jnp.where(left_live, lax.dynamic_index_in_dim(bcols, lower, 0, keepdims=False), -100)
    rrow = jnp.where(live, brows, -300).reshape(-1)
    rcol = jnp.where(live, bcols, -300).reshape(-1)
    meta = jnp.zeros((64, 128), jnp.int32)
    meta = meta.at[0:slot_count].set(jnp.broadcast_to(lrow[:, None], (slot_count, 128)))
    meta = meta.at[8:8 + slot_count].set(jnp.broadcast_to(lcol[:, None], (slot_count, 128)))
    meta = meta.at[16:16 + groups * slot_count].set(jnp.broadcast_to(rrow[:, None], (groups * slot_count, 128)))
    meta = meta.at[32:32 + groups * slot_count].set(jnp.broadcast_to(rcol[:, None], (groups * slot_count, 128)))
    meta = meta.at[48, :slot_count].set(left_places)
    meta = meta.at[49, : groups * slot_count].set(right_places)
    recv_l, recv_r, recv_ml, recv_mr, total_tile = exchange(blocks[0, 0], meta, row_count, col_count)
    totals = jnp.zeros((RB * width, groups * RB * width), jnp.float32)
    for step in range(STEPS):
        rp = recv_r[step].reshape(groups * slot_count, width, width)
        right_dense = densify(rp, recv_mr[step, 49, : groups * slot_count], RB, groups * RB)
        left_dense = densify(recv_l[step], recv_ml[step, 48, :slot_count], RB, RB)
        totals = totals + jnp.dot(left_dense, right_dense, preferred_element_type=jnp.float32)
    overall = total_tile[0, 0]
    trace_value = overall / math.sqrt(row_count * RB * width)
    return (totals.astype(jnp.bfloat16), trace_value)


def solution(mesh):
    return jax.shard_map(
        body,
        mesh=mesh,
        in_specs=(
            P("row", "col", None, None, None, None),
            P("row", "col", None, None),
            P("row", "col", None, None),
            P("row", "col", None),
        ),
        out_specs=(P("row", "col"), P()),
        check_vma=False,
    )
```

```python
import functools
import math

import jax
import jax.numpy as jnp
from jax import lax
from jax.experimental import pallas as pl
from jax.experimental.pallas import tpu as pltpu
from jax.sharding import PartitionSpec as P

RB = 5
STEPS = 4
MESH = pl.DeviceIdType.MESH


def densify(pieces, places, nrows, ncols):
    width = pieces.shape[-1]
    count = pieces.shape[0]
    onehot = (places[None, :] == jnp.arange(nrows * ncols, dtype=jnp.int32)[:, None]).astype(
        pieces.dtype
    )
    dense = jnp.dot(
        onehot, pieces.reshape(count, width * width), preferred_element_type=jnp.float32
    )
    dense = dense.reshape(nrows, ncols, width, width).transpose(0, 2, 1, 3)
    return dense.reshape(nrows * width, ncols * width).astype(pieces.dtype)


def exchange_kernel(row_count, col_count, groups, blocks_ref, meta_ref, *refs):
    recv_l, recv_r, recv_ml, recv_mr = (refs[i * STEPS:(i + 1) * STEPS] for i in range(4))
    send_sem, recv_sem = refs[4 * STEPS:]
    r = lax.axis_index("row")
    c = lax.axis_index("col")
    a = r // groups
    b = r % groups

    def l_self(s):
        return (a + s) % col_count == 0

    def r_self(s):
        return (c + s) % col_count == 0

    def l_at(shift):
        return (r, (c + shift + 4 * col_count) % col_count)

    def r_at(shift):
        return ((r + shift + 4 * row_count) % row_count, c)

    left_plan, right_plan = {}, {}
    left_plan[1] = (l_self(1), l_at(-(a + 1)), l_at(a + 1))
    right_plan[1] = (r_self(1), r_at(-groups * (c + 1)), r_at(groups * (c + 1)))
    for s in (0, 2, 3):
        left_plan[s] = (l_self(s), l_at(1 - s), l_at(s - 1))
        right_plan[s] = (r_self(s), r_at(groups * (1 - s)), r_at(groups * (s - 1)))

    barrier = pltpu.get_barrier_semaphore()
    peers = 0
    for plan in (left_plan, right_plan):
        for s in range(STEPS):
            is_self, dst, src = plan[s]

            @pl.when(jnp.logical_not(is_self))
            def _(dst=dst, src=src):
                pl.semaphore_signal(barrier, 1, device_id=dst, device_id_type=MESH)
                pl.semaphore_signal(barrier, 1, device_id=src, device_id_type=MESH)

            peers = peers + jnp.where(is_self, 0, 2)
    pl.semaphore_wait(barrier, peers)

    sides = [
        (left_plan, meta_ref, lambda s: recv_ml[s]),
        (right_plan, meta_ref, lambda s: recv_mr[s]),
        (left_plan, blocks_ref.at[b], lambda s: recv_l[s]),
    ]
    for g in range(groups):
        sides.append((right_plan, blocks_ref.at[g], lambda s, g=g: recv_r[s].at[g]))
    kinds = len(sides)

    def transfer(plan, s, source, target, j):
        is_self, dst, _ = plan[s]
        k = kinds * s + j
        local = pltpu.make_async_copy(source, target, recv_sem.at[k])
        remote = pltpu.make_async_remote_copy(
            source, target, send_sem.at[k], recv_sem.at[k],
            device_id=dst, device_id_type=MESH,
        )
        return is_self, local, remote

    def finish_recv(job):
        is_self, local, remote = job

        @pl.when(is_self)
        def _():
            local.wait()

        @pl.when(jnp.logical_not(is_self))
        def _():
            remote.wait_recv()

    firsts = []
    for j, (plan, source, target) in enumerate(sides):
        job = transfer(plan, 1, source, target(1), j)
        firsts.append(job)
        is_self, local, remote = job

        @pl.when(is_self)
        def _(local=local):
            local.start()

        @pl.when(jnp.logical_not(is_self))
        def _(remote=remote):
            remote.start()

    for j, (plan, source, target) in enumerate(sides):
        for s in (0, 2, 3):
            is_self, local, remote = transfer(plan, s, source, target(s), j)

            @pl.when(is_self)
            def _(local=local):
                local.start()

    forwards = []
    for j, (plan, source, target) in enumerate(sides):
        finish_recv(firsts[j])
        for s in (0, 2, 3):
            job = transfer(plan, s, target(1), target(s), j)
            forwards.append(job)
            is_self, local, remote = job

            @pl.when(jnp.logical_not(is_self))
            def _(remote=remote):
                remote.start()

    for job in forwards:
        finish_recv(job)
    for is_self, local, remote in firsts + forwards:
        @pl.when(jnp.logical_not(is_self))
        def _(remote=remote):
            remote.wait_send()


def exchange(blocks, meta, row_count, col_count):
    groups, slots, width = blocks.shape[0], blocks.shape[1], blocks.shape[2]
    vmem = pl.BlockSpec(memory_space=pltpu.VMEM)
    return pl.pallas_call(
        functools.partial(exchange_kernel, row_count, col_count, groups),
        out_shape=(
            [jax.ShapeDtypeStruct((slots, width, width), blocks.dtype)] * STEPS
            + [jax.ShapeDtypeStruct((groups, slots, width, width), blocks.dtype)] * STEPS
            + [jax.ShapeDtypeStruct(meta.shape, meta.dtype)] * (2 * STEPS)
        ),
        in_specs=[vmem, vmem],
        out_specs=[vmem] * (4 * STEPS),
        scratch_shapes=[
            pltpu.SemaphoreType.DMA(((3 + groups) * STEPS,)),
            pltpu.SemaphoreType.DMA(((3 + groups) * STEPS,)),
        ],
        compiler_params=pltpu.CompilerParams(collective_id=0, has_side_effects=True),
    )(blocks, meta)


def trace_kernel(row_count, col_count, groups,
                 term_ref, out_ref, row_buf, col_buf, send_sem, recv_sem, col_send, col_recv):
    r = lax.axis_index("row")
    c = lax.axis_index("col")
    diagonal = c == r // groups
    barrier = pltpu.get_barrier_semaphore()

    @pl.when(diagonal)
    def _():
        for cc in range(col_count):
            @pl.when(cc != c)
            def _(cc=cc):
                pl.semaphore_signal(barrier, 1, device_id=(r, cc), device_id_type=MESH)

    @pl.when(jnp.logical_not(diagonal))
    def _():
        pl.semaphore_signal(barrier, 1, device_id=(r, r // groups), device_id_type=MESH)

    for rr in range(row_count):
        @pl.when(rr != r)
        def _(rr=rr):
            pl.semaphore_signal(barrier, 1, device_id=(rr, c), device_id_type=MESH)

    pl.semaphore_wait(barrier, (row_count - 1) + jnp.where(diagonal, col_count - 1, 1))

    row_copies = []
    for cc in range(col_count):
        row_copies.append(pltpu.make_async_remote_copy(
            term_ref, row_buf, send_sem.at[cc], recv_sem.at[0],
            device_id=(r, cc), device_id_type=MESH,
        ))

    @pl.when(diagonal)
    def _():
        for cc in range(col_count):
            @pl.when(cc != c)
            def _(cc=cc):
                row_copies[cc].start()

    @pl.when(jnp.logical_not(diagonal))
    def _():
        row_copies[0].wait_recv()

    def col_copy(source, rr):
        return pltpu.make_async_remote_copy(
            source, col_buf.at[r], col_send.at[rr], col_recv.at[r],
            device_id=(rr, c), device_id_type=MESH,
        )

    for source, chosen in ((term_ref, diagonal), (row_buf, jnp.logical_not(diagonal))):
        @pl.when(chosen)
        def _(source=source):
            for rr in range(row_count):
                @pl.when(rr != r)
                def _(rr=rr):
                    col_copy(source, rr).start()

    for rr in range(row_count):
        @pl.when(rr != r)
        def _(rr=rr):
            pltpu.make_async_remote_copy(
                term_ref, col_buf.at[rr], col_send.at[rr], col_recv.at[rr],
                device_id=(rr, c), device_id_type=MESH,
            ).wait_recv()

    for source, chosen in ((term_ref, diagonal), (row_buf, jnp.logical_not(diagonal))):
        @pl.when(chosen)
        def _(source=source):
            for rr in range(row_count):
                @pl.when(rr != r)
                def _(rr=rr):
                    col_copy(source, rr).wait_send()
            col_buf[r] = source[...]

    @pl.when(diagonal)
    def _():
        for cc in range(col_count):
            @pl.when(cc != c)
            def _(cc=cc):
                row_copies[cc].wait_send()

    total = jnp.zeros(out_ref.shape, jnp.float32)
    for rr in range(row_count):
        total = total + col_buf[rr]
    out_ref[...] = total


def trace_total(term, row_count, col_count, groups):
    tile = jnp.broadcast_to(term, (8, 128))
    vmem = pl.BlockSpec(memory_space=pltpu.VMEM)
    out = pl.pallas_call(
        functools.partial(trace_kernel, row_count, col_count, groups),
        out_shape=jax.ShapeDtypeStruct((8, 128), jnp.float32),
        in_specs=[vmem],
        out_specs=vmem,
        scratch_shapes=[
            pltpu.VMEM((8, 128), jnp.float32),
            pltpu.VMEM((row_count, 8, 128), jnp.float32),
            pltpu.SemaphoreType.DMA((col_count,)),
            pltpu.SemaphoreType.DMA((1,)),
            pltpu.SemaphoreType.DMA((row_count,)),
            pltpu.SemaphoreType.DMA((row_count,)),
        ],
        compiler_params=pltpu.CompilerParams(collective_id=1, has_side_effects=True),
    )(tile)
    return out[0, 0]


def body(blocks, block_rows, block_cols, counts):
    groups = blocks.shape[2]
    slot_count = blocks.shape[3]
    width = blocks.shape[4]
    row_count = lax.axis_size("row")
    col_count = lax.axis_size("col")
    row_place = lax.axis_index("row")
    col_place = lax.axis_index("col")
    lower = row_place % groups
    filled = counts[0, 0]
    live = jnp.arange(slot_count, dtype=jnp.int32)[None, :] < filled[:, None]
    left_places_all = jnp.where(live, block_rows[0, 0] * RB + block_cols[0, 0], -1)
    offsets = (jnp.arange(groups, dtype=jnp.int32) * RB)[:, None]
    right_places = jnp.where(
        live, block_rows[0, 0] * (groups * RB) + block_cols[0, 0] + offsets, -1
    ).reshape(-1)
    left_places = lax.dynamic_index_in_dim(left_places_all, lower, 0, keepdims=False)
    meta = jnp.zeros((8, 128), jnp.int32)
    meta = meta.at[0, :slot_count].set(left_places)
    meta = meta.at[1, : groups * slot_count].set(right_places)
    received = exchange(blocks[0, 0], meta, row_count, col_count)
    recv_l, recv_r, recv_ml, recv_mr = (received[i * STEPS:(i + 1) * STEPS] for i in range(4))
    totals = jnp.zeros((RB * width, groups * RB * width), jnp.float32)
    for step in range(STEPS):
        rp = recv_r[step].reshape(groups * slot_count, width, width)
        right_dense = densify(rp, recv_mr[step][1, : groups * slot_count], RB, groups * RB)
        left_dense = densify(recv_l[step], recv_ml[step][0, :slot_count], RB, RB)
        totals = totals + jnp.dot(left_dense, right_dense, preferred_element_type=jnp.float32)
    shift_amount = row_place - groups * col_place
    valid = (shift_amount >= 0) & (shift_amount < groups)
    start = jnp.clip(shift_amount, 0, groups - 1) * RB * width
    window = lax.dynamic_slice_in_dim(totals, start, RB * width, 1)
    term = jnp.where(valid, jnp.trace(window), jnp.zeros((), jnp.float32))
    overall = trace_total(term, row_count, col_count, groups)
    trace_value = overall / math.sqrt(row_count * RB * width)
    return (totals.astype(jnp.bfloat16), trace_value)


def solution(mesh):
    return jax.shard_map(
        body,
        mesh=mesh,
        in_specs=(
            P("row", "col", None, None, None, None),
            P("row", "col", None, None),
            P("row", "col", None, None),
            P("row", "col", None),
        ),
        out_specs=(P("row", "col"), P()),
        check_vma=False,
    )
```

```python
import functools
import math

import jax
import jax.numpy as jnp
from jax import lax
from jax.experimental import pallas as pl
from jax.experimental.pallas import tpu as pltpu
from jax.sharding import PartitionSpec as P

RB = 5
STEPS = 4
MESH = pl.DeviceIdType.MESH


def densify(pieces, places, nrows, ncols):
    width = pieces.shape[-1]
    count = pieces.shape[0]
    onehot = (places[None, :] == jnp.arange(nrows * ncols, dtype=jnp.int32)[:, None]).astype(
        pieces.dtype
    )
    dense = jnp.dot(
        onehot, pieces.reshape(count, width * width), preferred_element_type=jnp.float32
    )
    dense = dense.reshape(nrows, ncols, width, width).transpose(0, 2, 1, 3)
    return dense.reshape(nrows * width, ncols * width).astype(pieces.dtype)


def exchange_kernel(row_count, col_count, groups,
                    blocks_ref, meta_ref, recv_l, recv_r, recv_ml, recv_mr, send_sem, recv_sem):
    r = lax.axis_index("row")
    c = lax.axis_index("col")
    a = r // groups
    b = r % groups

    def l_self(s):
        return (a + s) % col_count == 0

    def r_self(s):
        return (c + s) % col_count == 0

    def l_at(shift):
        return (r, (c + shift + 4 * col_count) % col_count)

    def r_at(shift):
        return ((r + shift + 4 * row_count) % row_count, c)

    left_plan, right_plan = {}, {}
    left_plan[1] = (l_self(1), l_at(-(a + 1)), l_at(a + 1))
    right_plan[1] = (r_self(1), r_at(-groups * (c + 1)), r_at(groups * (c + 1)))
    for s in (0, 2, 3):
        left_plan[s] = (l_self(s), l_at(1 - s), l_at(s - 1))
        right_plan[s] = (r_self(s), r_at(groups * (1 - s)), r_at(groups * (s - 1)))

    barrier = pltpu.get_barrier_semaphore()
    peers = 0
    for plan in (left_plan, right_plan):
        for s in range(STEPS):
            is_self, dst, src = plan[s]

            @pl.when(jnp.logical_not(is_self))
            def _(dst=dst, src=src):
                pl.semaphore_signal(barrier, 1, device_id=dst, device_id_type=MESH)
                pl.semaphore_signal(barrier, 1, device_id=src, device_id_type=MESH)

            peers = peers + jnp.where(is_self, 0, 2)
    pl.semaphore_wait(barrier, peers)

    sides = [
        (left_plan, meta_ref, lambda s: recv_ml.at[s]),
        (right_plan, meta_ref, lambda s: recv_mr.at[s]),
        (left_plan, blocks_ref.at[b], lambda s: recv_l.at[s]),
    ]
    for g in range(groups):
        sides.append((right_plan, blocks_ref.at[g], lambda s, g=g: recv_r.at[s, g]))
    kinds = len(sides)

    def transfer(plan, s, source, target, j):
        is_self, dst, _ = plan[s]
        k = kinds * s + j
        local = pltpu.make_async_copy(source, target, recv_sem.at[k])
        remote = pltpu.make_async_remote_copy(
            source, target, send_sem.at[k], recv_sem.at[k],
            device_id=dst, device_id_type=MESH,
        )
        return is_self, local, remote

    def finish_recv(job):
        is_self, local, remote = job

        @pl.when(is_self)
        def _():
            local.wait()

        @pl.when(jnp.logical_not(is_self))
        def _():
            remote.wait_recv()

    firsts = []
    for j, (plan, source, target) in enumerate(sides):
        job = transfer(plan, 1, source, target(1), j)
        firsts.append(job)
        is_self, local, remote = job

        @pl.when(is_self)
        def _(local=local):
            local.start()

        @pl.when(jnp.logical_not(is_self))
        def _(remote=remote):
            remote.start()

    for j, (plan, source, target) in enumerate(sides):
        for s in (0, 2, 3):
            is_self, local, remote = transfer(plan, s, source, target(s), j)

            @pl.when(is_self)
            def _(local=local):
                local.start()

    forwards = []
    for j, (plan, source, target) in enumerate(sides):
        finish_recv(firsts[j])
        for s in (0, 2, 3):
            job = transfer(plan, s, target(1), target(s), j)
            forwards.append(job)
            is_self, local, remote = job

            @pl.when(jnp.logical_not(is_self))
            def _(remote=remote):
                remote.start()

    for job in forwards:
        finish_recv(job)
    for is_self, local, remote in firsts + forwards:
        @pl.when(jnp.logical_not(is_self))
        def _(remote=remote):
            remote.wait_send()


def exchange(blocks, meta, row_count, col_count):
    groups, slots, width = blocks.shape[0], blocks.shape[1], blocks.shape[2]
    vmem = pl.BlockSpec(memory_space=pltpu.VMEM)
    return pl.pallas_call(
        functools.partial(exchange_kernel, row_count, col_count, groups),
        out_shape=(
            jax.ShapeDtypeStruct((STEPS, slots, width, width), blocks.dtype),
            jax.ShapeDtypeStruct((STEPS, groups, slots, width, width), blocks.dtype),
            jax.ShapeDtypeStruct((STEPS,) + meta.shape, meta.dtype),
            jax.ShapeDtypeStruct((STEPS,) + meta.shape, meta.dtype),
        ),
        in_specs=[vmem, vmem],
        out_specs=(vmem, vmem, vmem, vmem),
        scratch_shapes=[
            pltpu.SemaphoreType.DMA(((3 + groups) * STEPS,)),
            pltpu.SemaphoreType.DMA(((3 + groups) * STEPS,)),
        ],
        compiler_params=pltpu.CompilerParams(collective_id=0, has_side_effects=True),
    )(blocks, meta)


def trace_kernel(row_count, col_count, groups,
                 term_ref, out_ref, row_buf, col_buf, send_sem, recv_sem, col_send, col_recv):
    r = lax.axis_index("row")
    c = lax.axis_index("col")
    diagonal = c == r // groups
    barrier = pltpu.get_barrier_semaphore()

    @pl.when(diagonal)
    def _():
        for cc in range(col_count):
            @pl.when(cc != c)
            def _(cc=cc):
                pl.semaphore_signal(barrier, 1, device_id=(r, cc), device_id_type=MESH)

    @pl.when(jnp.logical_not(diagonal))
    def _():
        pl.semaphore_signal(barrier, 1, device_id=(r, r // groups), device_id_type=MESH)

    for rr in range(row_count):
        @pl.when(rr != r)
        def _(rr=rr):
            pl.semaphore_signal(barrier, 1, device_id=(rr, c), device_id_type=MESH)

    pl.semaphore_wait(barrier, (row_count - 1) + jnp.where(diagonal, col_count - 1, 1))

    row_copies = []
    for cc in range(col_count):
        row_copies.append(pltpu.make_async_remote_copy(
            term_ref, row_buf, send_sem.at[cc], recv_sem.at[0],
            device_id=(r, cc), device_id_type=MESH,
        ))

    @pl.when(diagonal)
    def _():
        for cc in range(col_count):
            @pl.when(cc != c)
            def _(cc=cc):
                row_copies[cc].start()

    @pl.when(jnp.logical_not(diagonal))
    def _():
        row_copies[0].wait_recv()

    def col_copy(source, rr):
        return pltpu.make_async_remote_copy(
            source, col_buf.at[r], col_send.at[rr], col_recv.at[r],
            device_id=(rr, c), device_id_type=MESH,
        )

    for source, chosen in ((term_ref, diagonal), (row_buf, jnp.logical_not(diagonal))):
        @pl.when(chosen)
        def _(source=source):
            for rr in range(row_count):
                @pl.when(rr != r)
                def _(rr=rr):
                    col_copy(source, rr).start()

    for rr in range(row_count):
        @pl.when(rr != r)
        def _(rr=rr):
            pltpu.make_async_remote_copy(
                term_ref, col_buf.at[rr], col_send.at[rr], col_recv.at[rr],
                device_id=(rr, c), device_id_type=MESH,
            ).wait_recv()

    for source, chosen in ((term_ref, diagonal), (row_buf, jnp.logical_not(diagonal))):
        @pl.when(chosen)
        def _(source=source):
            for rr in range(row_count):
                @pl.when(rr != r)
                def _(rr=rr):
                    col_copy(source, rr).wait_send()
            col_buf[r] = source[...]

    @pl.when(diagonal)
    def _():
        for cc in range(col_count):
            @pl.when(cc != c)
            def _(cc=cc):
                row_copies[cc].wait_send()

    total = jnp.zeros(out_ref.shape, jnp.float32)
    for rr in range(row_count):
        total = total + col_buf[rr]
    out_ref[...] = total


def trace_total(term, row_count, col_count, groups):
    tile = jnp.broadcast_to(term, (8, 128))
    vmem = pl.BlockSpec(memory_space=pltpu.VMEM)
    out = pl.pallas_call(
        functools.partial(trace_kernel, row_count, col_count, groups),
        out_shape=jax.ShapeDtypeStruct((8, 128), jnp.float32),
        in_specs=[vmem],
        out_specs=vmem,
        scratch_shapes=[
            pltpu.VMEM((8, 128), jnp.float32),
            pltpu.VMEM((row_count, 8, 128), jnp.float32),
            pltpu.SemaphoreType.DMA((col_count,)),
            pltpu.SemaphoreType.DMA((1,)),
            pltpu.SemaphoreType.DMA((row_count,)),
            pltpu.SemaphoreType.DMA((row_count,)),
        ],
        compiler_params=pltpu.CompilerParams(collective_id=1, has_side_effects=True),
    )(tile)
    return out[0, 0]


def body(blocks, block_rows, block_cols, counts):
    groups = blocks.shape[2]
    slot_count = blocks.shape[3]
    width = blocks.shape[4]
    row_count = lax.axis_size("row")
    col_count = lax.axis_size("col")
    row_place = lax.axis_index("row")
    col_place = lax.axis_index("col")
    lower = row_place % groups
    filled = counts[0, 0]
    live = jnp.arange(slot_count, dtype=jnp.int32)[None, :] < filled[:, None]
    left_places_all = jnp.where(live, block_rows[0, 0] * RB + block_cols[0, 0], -1)
    offsets = (jnp.arange(groups, dtype=jnp.int32) * RB)[:, None]
    right_places = jnp.where(
        live, block_rows[0, 0] * (groups * RB) + block_cols[0, 0] + offsets, -1
    ).reshape(-1)
    left_places = lax.dynamic_index_in_dim(left_places_all, lower, 0, keepdims=False)
    meta = jnp.zeros((8, 128), jnp.int32)
    meta = meta.at[0, :slot_count].set(left_places)
    meta = meta.at[1, : groups * slot_count].set(right_places)
    recv_l, recv_r, recv_ml, recv_mr = exchange(blocks[0, 0], meta, row_count, col_count)
    cells = jnp.arange(RB * RB, dtype=jnp.int32)
    left_hot = (recv_ml[:, 0, None, :slot_count] == cells[None, :, None]).astype(blocks.dtype)
    left_dense = jnp.einsum(
        "sct,stk->sck", left_hot, recv_l.reshape(STEPS, slot_count, width * width),
        preferred_element_type=jnp.float32,
    ).astype(blocks.dtype)
    left_dense = left_dense.reshape(STEPS, RB, RB, width, width).transpose(1, 3, 0, 2, 4)
    left_dense = left_dense.reshape(RB * width, STEPS * RB * width)
    cells = jnp.arange(RB * groups * RB, dtype=jnp.int32)
    right_hot = (
        recv_mr[:, 1, None, : groups * slot_count] == cells[None, :, None]
    ).astype(blocks.dtype)
    right_dense = jnp.einsum(
        "sct,stk->sck", right_hot,
        recv_r.reshape(STEPS, groups * slot_count, width * width),
        preferred_element_type=jnp.float32,
    ).astype(blocks.dtype)
    right_dense = right_dense.reshape(STEPS, RB, groups * RB, width, width).transpose(0, 1, 3, 2, 4)
    right_dense = right_dense.reshape(STEPS * RB * width, groups * RB * width)
    totals = jnp.dot(left_dense, right_dense, preferred_element_type=jnp.float32)
    shift_amount = row_place - groups * col_place
    valid = (shift_amount >= 0) & (shift_amount < groups)
    start = jnp.clip(shift_amount, 0, groups - 1) * RB * width
    window = lax.dynamic_slice_in_dim(totals, start, RB * width, 1)
    term = jnp.where(valid, jnp.trace(window), jnp.zeros((), jnp.float32))
    overall = trace_total(term, row_count, col_count, groups)
    trace_value = overall / math.sqrt(row_count * RB * width)
    return (totals.astype(jnp.bfloat16), trace_value)


def solution(mesh):
    return jax.shard_map(
        body,
        mesh=mesh,
        in_specs=(
            P("row", "col", None, None, None, None),
            P("row", "col", None, None),
            P("row", "col", None, None),
            P("row", "col", None),
        ),
        out_specs=(P("row", "col"), P()),
        check_vma=False,
    )
```

```python
import functools
import math

import jax
import jax.numpy as jnp
from jax import lax
from jax.experimental import pallas as pl
from jax.experimental.pallas import tpu as pltpu
from jax.sharding import PartitionSpec as P

RB = 5
STEPS = 4
MESH = pl.DeviceIdType.MESH


def densify(pieces, places, nrows, ncols):
    width = pieces.shape[-1]
    count = pieces.shape[0]
    onehot = (places[None, :] == jnp.arange(nrows * ncols, dtype=jnp.int32)[:, None]).astype(
        pieces.dtype
    )
    dense = jnp.dot(
        onehot, pieces.reshape(count, width * width), preferred_element_type=jnp.float32
    )
    dense = dense.reshape(nrows, ncols, width, width).transpose(0, 2, 1, 3)
    return dense.reshape(nrows * width, ncols * width).astype(pieces.dtype)


def exchange_kernel(row_count, col_count, groups,
                    blocks_ref, meta_ref, recv_l, recv_r, recv_ml, recv_mr, send_sem, recv_sem):
    r = lax.axis_index("row")
    c = lax.axis_index("col")
    a = r // groups
    b = r % groups
    slots_per_group = blocks_ref.shape[1]

    def l_self(s):
        return (a + s) % col_count == 0

    def r_self(s):
        return (c + s) % col_count == 0

    def l_at(shift):
        return (r, (c + shift + 4 * col_count) % col_count)

    def r_at(shift):
        return ((r + shift + 4 * row_count) % row_count, c)

    left_plan, right_plan = {}, {}
    left_plan[1] = (l_self(1), l_at(-(a + 1)), l_at(a + 1))
    right_plan[1] = (r_self(1), r_at(-groups * (c + 1)), r_at(groups * (c + 1)))
    for s in (0, 2, 3):
        left_plan[s] = (l_self(s), l_at(1 - s), l_at(s - 1))
        right_plan[s] = (r_self(s), r_at(groups * (1 - s)), r_at(groups * (s - 1)))

    barrier = pltpu.get_barrier_semaphore()
    peers = 0
    for plan in (left_plan, right_plan):
        for s in range(STEPS):
            is_self, dst, src = plan[s]

            @pl.when(jnp.logical_not(is_self))
            def _(dst=dst, src=src):
                pl.semaphore_signal(barrier, 1, device_id=dst, device_id_type=MESH)
                pl.semaphore_signal(barrier, 1, device_id=src, device_id_type=MESH)

            peers = peers + jnp.where(is_self, 0, 2)
    pl.semaphore_wait(barrier, peers)

    half = slots_per_group // 2
    sides = [
        (left_plan, meta_ref, lambda s: recv_ml.at[s]),
        (right_plan, meta_ref, lambda s: recv_mr.at[s]),
    ]
    for h in range(2):
        part = pl.ds(h * half, half)
        sides.append((left_plan, blocks_ref.at[b, part], lambda s, part=part: recv_l.at[s, part]))
    for g in range(groups):
        for h in range(2):
            part = pl.ds(h * half, half)
            sides.append((right_plan, blocks_ref.at[g, part],
                          lambda s, g=g, part=part: recv_r.at[s, g, part]))
    kinds = len(sides)

    def transfer(plan, s, source, target, j):
        is_self, dst, _ = plan[s]
        k = kinds * s + j
        local = pltpu.make_async_copy(source, target, recv_sem.at[k])
        remote = pltpu.make_async_remote_copy(
            source, target, send_sem.at[k], recv_sem.at[k],
            device_id=dst, device_id_type=MESH,
        )
        return is_self, local, remote

    def finish_recv(job):
        is_self, local, remote = job

        @pl.when(is_self)
        def _():
            local.wait()

        @pl.when(jnp.logical_not(is_self))
        def _():
            remote.wait_recv()

    firsts = []
    for j, (plan, source, target) in enumerate(sides):
        job = transfer(plan, 1, source, target(1), j)
        firsts.append(job)
        is_self, local, remote = job

        @pl.when(is_self)
        def _(local=local):
            local.start()

        @pl.when(jnp.logical_not(is_self))
        def _(remote=remote):
            remote.start()

    for j, (plan, source, target) in enumerate(sides):
        for s in (0, 2, 3):
            is_self, local, remote = transfer(plan, s, source, target(s), j)

            @pl.when(is_self)
            def _(local=local):
                local.start()

    forwards = []
    for j, (plan, source, target) in enumerate(sides):
        finish_recv(firsts[j])
        for s in (0, 2, 3):
            job = transfer(plan, s, target(1), target(s), j)
            forwards.append(job)
            is_self, local, remote = job

            @pl.when(jnp.logical_not(is_self))
            def _(remote=remote):
                remote.start()

    for job in forwards:
        finish_recv(job)
    for is_self, local, remote in firsts + forwards:
        @pl.when(jnp.logical_not(is_self))
        def _(remote=remote):
            remote.wait_send()


def exchange(blocks, meta, row_count, col_count):
    groups, slots, width = blocks.shape[0], blocks.shape[1], blocks.shape[2]
    vmem = pl.BlockSpec(memory_space=pltpu.VMEM)
    return pl.pallas_call(
        functools.partial(exchange_kernel, row_count, col_count, groups),
        out_shape=(
            jax.ShapeDtypeStruct((STEPS, slots, width, width), blocks.dtype),
            jax.ShapeDtypeStruct((STEPS, groups, slots, width, width), blocks.dtype),
            jax.ShapeDtypeStruct((STEPS,) + meta.shape, meta.dtype),
            jax.ShapeDtypeStruct((STEPS,) + meta.shape, meta.dtype),
        ),
        in_specs=[vmem, vmem],
        out_specs=(vmem, vmem, vmem, vmem),
        scratch_shapes=[
            pltpu.SemaphoreType.DMA(((4 + 2 * groups) * STEPS,)),
            pltpu.SemaphoreType.DMA(((4 + 2 * groups) * STEPS,)),
        ],
        compiler_params=pltpu.CompilerParams(collective_id=0, has_side_effects=True),
    )(blocks, meta)


def trace_kernel(row_count, col_count, groups,
                 term_ref, out_ref, row_buf, col_buf, send_sem, recv_sem, col_send, col_recv):
    r = lax.axis_index("row")
    c = lax.axis_index("col")
    diagonal = c == r // groups
    barrier = pltpu.get_barrier_semaphore()

    @pl.when(diagonal)
    def _():
        for cc in range(col_count):
            @pl.when(cc != c)
            def _(cc=cc):
                pl.semaphore_signal(barrier, 1, device_id=(r, cc), device_id_type=MESH)

    @pl.when(jnp.logical_not(diagonal))
    def _():
        pl.semaphore_signal(barrier, 1, device_id=(r, r // groups), device_id_type=MESH)

    for rr in range(row_count):
        @pl.when(rr != r)
        def _(rr=rr):
            pl.semaphore_signal(barrier, 1, device_id=(rr, c), device_id_type=MESH)

    pl.semaphore_wait(barrier, (row_count - 1) + jnp.where(diagonal, col_count - 1, 1))

    row_copies = []
    for cc in range(col_count):
        row_copies.append(pltpu.make_async_remote_copy(
            term_ref, row_buf, send_sem.at[cc], recv_sem.at[0],
            device_id=(r, cc), device_id_type=MESH,
        ))

    @pl.when(diagonal)
    def _():
        for cc in range(col_count):
            @pl.when(cc != c)
            def _(cc=cc):
                row_copies[cc].start()

    @pl.when(jnp.logical_not(diagonal))
    def _():
        row_copies[0].wait_recv()

    def col_copy(source, rr):
        return pltpu.make_async_remote_copy(
            source, col_buf.at[r], col_send.at[rr], col_recv.at[r],
            device_id=(rr, c), device_id_type=MESH,
        )

    for source, chosen in ((term_ref, diagonal), (row_buf, jnp.logical_not(diagonal))):
        @pl.when(chosen)
        def _(source=source):
            for rr in range(row_count):
                @pl.when(rr != r)
                def _(rr=rr):
                    col_copy(source, rr).start()

    for rr in range(row_count):
        @pl.when(rr != r)
        def _(rr=rr):
            pltpu.make_async_remote_copy(
                term_ref, col_buf.at[rr], col_send.at[rr], col_recv.at[rr],
                device_id=(rr, c), device_id_type=MESH,
            ).wait_recv()

    for source, chosen in ((term_ref, diagonal), (row_buf, jnp.logical_not(diagonal))):
        @pl.when(chosen)
        def _(source=source):
            for rr in range(row_count):
                @pl.when(rr != r)
                def _(rr=rr):
                    col_copy(source, rr).wait_send()
            col_buf[r] = source[...]

    @pl.when(diagonal)
    def _():
        for cc in range(col_count):
            @pl.when(cc != c)
            def _(cc=cc):
                row_copies[cc].wait_send()

    total = jnp.zeros(out_ref.shape, jnp.float32)
    for rr in range(row_count):
        total = total + col_buf[rr]
    out_ref[...] = total


def trace_total(term, row_count, col_count, groups):
    tile = jnp.broadcast_to(term, (8, 128))
    vmem = pl.BlockSpec(memory_space=pltpu.VMEM)
    out = pl.pallas_call(
        functools.partial(trace_kernel, row_count, col_count, groups),
        out_shape=jax.ShapeDtypeStruct((8, 128), jnp.float32),
        in_specs=[vmem],
        out_specs=vmem,
        scratch_shapes=[
            pltpu.VMEM((8, 128), jnp.float32),
            pltpu.VMEM((row_count, 8, 128), jnp.float32),
            pltpu.SemaphoreType.DMA((col_count,)),
            pltpu.SemaphoreType.DMA((1,)),
            pltpu.SemaphoreType.DMA((row_count,)),
            pltpu.SemaphoreType.DMA((row_count,)),
        ],
        compiler_params=pltpu.CompilerParams(collective_id=1, has_side_effects=True),
    )(tile)
    return out[0, 0]


def body(blocks, block_rows, block_cols, counts):
    groups = blocks.shape[2]
    slot_count = blocks.shape[3]
    width = blocks.shape[4]
    row_count = lax.axis_size("row")
    col_count = lax.axis_size("col")
    row_place = lax.axis_index("row")
    col_place = lax.axis_index("col")
    lower = row_place % groups
    filled = counts[0, 0]
    live = jnp.arange(slot_count, dtype=jnp.int32)[None, :] < filled[:, None]
    left_places_all = jnp.where(live, block_rows[0, 0] * RB + block_cols[0, 0], -1)
    offsets = (jnp.arange(groups, dtype=jnp.int32) * RB)[:, None]
    right_places = jnp.where(
        live, block_rows[0, 0] * (groups * RB) + block_cols[0, 0] + offsets, -1
    ).reshape(-1)
    left_places = lax.dynamic_index_in_dim(left_places_all, lower, 0, keepdims=False)
    meta = jnp.zeros((8, 128), jnp.int32)
    meta = meta.at[0, :slot_count].set(left_places)
    meta = meta.at[1, : groups * slot_count].set(right_places)
    recv_l, recv_r, recv_ml, recv_mr = exchange(blocks[0, 0], meta, row_count, col_count)
    totals = jnp.zeros((RB * width, groups * RB * width), jnp.float32)
    for step in range(STEPS):
        rp = recv_r[step].reshape(groups * slot_count, width, width)
        right_dense = densify(rp, recv_mr[step, 1, : groups * slot_count], RB, groups * RB)
        left_dense = densify(recv_l[step], recv_ml[step, 0, :slot_count], RB, RB)
        totals = totals + jnp.dot(left_dense, right_dense, preferred_element_type=jnp.float32)
    shift_amount = row_place - groups * col_place
    valid = (shift_amount >= 0) & (shift_amount < groups)
    start = jnp.clip(shift_amount, 0, groups - 1) * RB * width
    window = lax.dynamic_slice_in_dim(totals, start, RB * width, 1)
    term = jnp.where(valid, jnp.trace(window), jnp.zeros((), jnp.float32))
    overall = trace_total(term, row_count, col_count, groups)
    trace_value = overall / math.sqrt(row_count * RB * width)
    return (totals.astype(jnp.bfloat16), trace_value)


def solution(mesh):
    return jax.shard_map(
        body,
        mesh=mesh,
        in_specs=(
            P("row", "col", None, None, None, None),
            P("row", "col", None, None),
            P("row", "col", None, None),
            P("row", "col", None),
        ),
        out_specs=(P("row", "col"), P()),
        check_vma=False,
    )
```

```python
import functools
import math

import jax
import jax.numpy as jnp
from jax import lax
from jax.experimental import pallas as pl
from jax.experimental.pallas import tpu as pltpu
from jax.sharding import PartitionSpec as P

RB = 5
STEPS = 4
MESH = pl.DeviceIdType.MESH


def densify(pieces, places, nrows, ncols):
    width = pieces.shape[-1]
    count = pieces.shape[0]
    onehot = (places[None, :] == jnp.arange(nrows * ncols, dtype=jnp.int32)[:, None]).astype(
        pieces.dtype
    )
    dense = jnp.dot(
        onehot, pieces.reshape(count, width * width), preferred_element_type=jnp.float32
    )
    dense = dense.reshape(nrows, ncols, width, width).transpose(0, 2, 1, 3)
    return dense.reshape(nrows * width, ncols * width).astype(pieces.dtype)


def exchange_kernel(row_count, col_count, groups,
                    blocks_ref, meta_ref, recv_l, recv_r, recv_ml, recv_mr, send_sem, recv_sem):
    r = lax.axis_index("row")
    c = lax.axis_index("col")
    a = r // groups
    b = r % groups

    def l_self(s):
        return (a + s) % col_count == 0

    def r_self(s):
        return (c + s) % col_count == 0

    def l_at(shift):
        return (r, (c + shift + 4 * col_count) % col_count)

    def r_at(shift):
        return ((r + shift + 4 * row_count) % row_count, c)

    left_plan, right_plan = {}, {}
    left_plan[1] = (l_self(1), l_at(-(a + 1)), l_at(a + 1))
    right_plan[1] = (r_self(1), r_at(-groups * (c + 1)), r_at(groups * (c + 1)))
    for s in (0, 2, 3):
        left_plan[s] = (l_self(s), l_at(1 - s), l_at(s - 1))
        right_plan[s] = (r_self(s), r_at(groups * (1 - s)), r_at(groups * (s - 1)))

    barrier = pltpu.get_barrier_semaphore()
    peers = 0
    for plan in (left_plan, right_plan):
        for s in range(STEPS):
            is_self, dst, src = plan[s]

            @pl.when(jnp.logical_not(is_self))
            def _(dst=dst, src=src):
                pl.semaphore_signal(barrier, 1, device_id=dst, device_id_type=MESH)
                pl.semaphore_signal(barrier, 1, device_id=src, device_id_type=MESH)

            peers = peers + jnp.where(is_self, 0, 2)
    pl.semaphore_wait(barrier, peers)

    sides = [
        (left_plan, meta_ref, lambda s: recv_ml.at[s]),
        (right_plan, meta_ref, lambda s: recv_mr.at[s]),
        (left_plan, blocks_ref.at[b], lambda s: recv_l.at[s]),
    ]
    for g in range(groups):
        sides.append((right_plan, blocks_ref.at[g], lambda s, g=g: recv_r.at[s, g]))
    kinds = len(sides)

    def transfer(plan, s, source, target, j):
        is_self, dst, _ = plan[s]
        k = kinds * s + j
        local = pltpu.make_async_copy(source, target, recv_sem.at[k])
        remote = pltpu.make_async_remote_copy(
            source, target, send_sem.at[k], recv_sem.at[k],
            device_id=dst, device_id_type=MESH,
        )
        return is_self, local, remote

    def finish_recv(job):
        is_self, local, remote = job

        @pl.when(is_self)
        def _():
            local.wait()

        @pl.when(jnp.logical_not(is_self))
        def _():
            remote.wait_recv()

    firsts = []
    for j, (plan, source, target) in enumerate(sides):
        job = transfer(plan, 1, source, target(1), j)
        firsts.append(job)
        is_self, local, remote = job

        @pl.when(is_self)
        def _(local=local):
            local.start()

        @pl.when(jnp.logical_not(is_self))
        def _(remote=remote):
            remote.start()

    for j, (plan, source, target) in enumerate(sides):
        for s in (0, 2, 3):
            is_self, local, remote = transfer(plan, s, source, target(s), j)

            @pl.when(is_self)
            def _(local=local):
                local.start()

    forwards = []
    for j, (plan, source, target) in enumerate(sides):
        finish_recv(firsts[j])
        for s in (0, 2, 3):
            job = transfer(plan, s, target(1), target(s), j)
            forwards.append(job)
            is_self, local, remote = job

            @pl.when(jnp.logical_not(is_self))
            def _(remote=remote):
                remote.start()

    for job in forwards:
        finish_recv(job)
    for is_self, local, remote in firsts + forwards:
        @pl.when(jnp.logical_not(is_self))
        def _(remote=remote):
            remote.wait_send()


def exchange(blocks, meta, row_count, col_count):
    groups, slots, width = blocks.shape[0], blocks.shape[1], blocks.shape[2]
    vmem = pl.BlockSpec(memory_space=pltpu.VMEM)
    return pl.pallas_call(
        functools.partial(exchange_kernel, row_count, col_count, groups),
        out_shape=(
            jax.ShapeDtypeStruct((STEPS, slots, width, width), blocks.dtype),
            jax.ShapeDtypeStruct((STEPS, groups, slots, width, width), blocks.dtype),
            jax.ShapeDtypeStruct((STEPS,) + meta.shape, meta.dtype),
            jax.ShapeDtypeStruct((STEPS,) + meta.shape, meta.dtype),
        ),
        in_specs=[vmem, vmem],
        out_specs=(vmem, vmem, vmem, vmem),
        scratch_shapes=[
            pltpu.SemaphoreType.DMA(((3 + groups) * STEPS,)),
            pltpu.SemaphoreType.DMA(((3 + groups) * STEPS,)),
        ],
        compiler_params=pltpu.CompilerParams(collective_id=0, has_side_effects=True),
    )(blocks, meta)


def trace_kernel(row_count, col_count, groups, *refs):
    lefts = refs[:STEPS]
    rights = refs[STEPS:2 * STEPS]
    (square_ref, out_ref, term_ref, acc, row_buf, col_buf,
     send_sem, recv_sem, col_send, col_recv) = refs[2 * STEPS:]
    r = lax.axis_index("row")
    c = lax.axis_index("col")
    diagonal = c == r // groups
    barrier = pltpu.get_barrier_semaphore()

    @pl.when(diagonal)
    def _():
        for cc in range(col_count):
            @pl.when(cc != c)
            def _(cc=cc):
                pl.semaphore_signal(barrier, 1, device_id=(r, cc), device_id_type=MESH)

    @pl.when(jnp.logical_not(diagonal))
    def _():
        pl.semaphore_signal(barrier, 1, device_id=(r, r // groups), device_id_type=MESH)

    for rr in range(row_count):
        @pl.when(rr != r)
        def _(rr=rr):
            pl.semaphore_signal(barrier, 1, device_id=(rr, c), device_id_type=MESH)

    rows = lefts[0].shape[0]
    cols = rights[0].shape[1]
    tile = 256 if cols % 256 == 0 else cols
    acc[...] = jnp.zeros(acc.shape, jnp.float32)
    for s in range(STEPS):
        @pl.loop(0, cols // tile)
        def _(j, s=s):
            span = pl.ds(pl.multiple_of(j * tile, tile), tile)
            acc[:, span] += jnp.dot(
                lefts[s][...], rights[s][:, span], preferred_element_type=jnp.float32)
    square_ref[...] = acc[...].astype(square_ref.dtype)
    shift = jnp.clip(r - groups * c, 0, groups - 1)
    window = acc[:, pl.ds(pl.multiple_of(shift * rows, 128), rows)]
    eye = (lax.broadcasted_iota(jnp.int32, (rows, rows), 0)
           == lax.broadcasted_iota(jnp.int32, (rows, rows), 1))
    term = jnp.sum(jnp.where(eye, window, 0.0), keepdims=True)
    term_ref[...] = jnp.broadcast_to(jnp.where(diagonal, term, 0.0), term_ref.shape)

    pl.semaphore_wait(barrier, (row_count - 1) + jnp.where(diagonal, col_count - 1, 1))

    row_copies = []
    for cc in range(col_count):
        row_copies.append(pltpu.make_async_remote_copy(
            term_ref, row_buf, send_sem.at[cc], recv_sem.at[0],
            device_id=(r, cc), device_id_type=MESH,
        ))

    @pl.when(diagonal)
    def _():
        for cc in range(col_count):
            @pl.when(cc != c)
            def _(cc=cc):
                row_copies[cc].start()

    @pl.when(jnp.logical_not(diagonal))
    def _():
        row_copies[0].wait_recv()

    def col_copy(source, rr):
        return pltpu.make_async_remote_copy(
            source, col_buf.at[r], col_send.at[rr], col_recv.at[r],
            device_id=(rr, c), device_id_type=MESH,
        )

    for source, chosen in ((term_ref, diagonal), (row_buf, jnp.logical_not(diagonal))):
        @pl.when(chosen)
        def _(source=source):
            for rr in range(row_count):
                @pl.when(rr != r)
                def _(rr=rr):
                    col_copy(source, rr).start()

    for rr in range(row_count):
        @pl.when(rr != r)
        def _(rr=rr):
            pltpu.make_async_remote_copy(
                term_ref, col_buf.at[rr], col_send.at[rr], col_recv.at[rr],
                device_id=(rr, c), device_id_type=MESH,
            ).wait_recv()

    for source, chosen in ((term_ref, diagonal), (row_buf, jnp.logical_not(diagonal))):
        @pl.when(chosen)
        def _(source=source):
            for rr in range(row_count):
                @pl.when(rr != r)
                def _(rr=rr):
                    col_copy(source, rr).wait_send()
            col_buf[r] = source[...]

    @pl.when(diagonal)
    def _():
        for cc in range(col_count):
            @pl.when(cc != c)
            def _(cc=cc):
                row_copies[cc].wait_send()

    total = jnp.zeros(out_ref.shape, jnp.float32)
    for rr in range(row_count):
        total = total + col_buf[rr]
    out_ref[...] = total


def finish(lefts, rights, row_count, col_count, groups):
    rows, cols = lefts[0].shape[0], rights[0].shape[1]
    vmem = pl.BlockSpec(memory_space=pltpu.VMEM)
    square, total = pl.pallas_call(
        functools.partial(trace_kernel, row_count, col_count, groups),
        out_shape=(
            jax.ShapeDtypeStruct((rows, cols), lefts[0].dtype),
            jax.ShapeDtypeStruct((8, 128), jnp.float32),
        ),
        in_specs=[vmem] * (2 * STEPS),
        out_specs=(vmem, vmem),
        scratch_shapes=[
            pltpu.VMEM((8, 128), jnp.float32),
            pltpu.VMEM((rows, cols), jnp.float32),
            pltpu.VMEM((8, 128), jnp.float32),
            pltpu.VMEM((row_count, 8, 128), jnp.float32),
            pltpu.SemaphoreType.DMA((col_count,)),
            pltpu.SemaphoreType.DMA((1,)),
            pltpu.SemaphoreType.DMA((row_count,)),
            pltpu.SemaphoreType.DMA((row_count,)),
        ],
        compiler_params=pltpu.CompilerParams(collective_id=1, has_side_effects=True),
    )(*lefts, *rights)
    return square, total[0, 0]


def body(blocks, block_rows, block_cols, counts):
    groups = blocks.shape[2]
    slot_count = blocks.shape[3]
    width = blocks.shape[4]
    row_count = lax.axis_size("row")
    col_count = lax.axis_size("col")
    row_place = lax.axis_index("row")
    col_place = lax.axis_index("col")
    lower = row_place % groups
    filled = counts[0, 0]
    live = jnp.arange(slot_count, dtype=jnp.int32)[None, :] < filled[:, None]
    left_places_all = jnp.where(live, block_rows[0, 0] * RB + block_cols[0, 0], -1)
    offsets = (jnp.arange(groups, dtype=jnp.int32) * RB)[:, None]
    right_places = jnp.where(
        live, block_rows[0, 0] * (groups * RB) + block_cols[0, 0] + offsets, -1
    ).reshape(-1)
    left_places = lax.dynamic_index_in_dim(left_places_all, lower, 0, keepdims=False)
    meta = jnp.zeros((8, 128), jnp.int32)
    meta = meta.at[0, :slot_count].set(left_places)
    meta = meta.at[1, : groups * slot_count].set(right_places)
    recv_l, recv_r, recv_ml, recv_mr = exchange(blocks[0, 0], meta, row_count, col_count)
    lefts, rights = [], []
    for step in range(STEPS):
        rp = recv_r[step].reshape(groups * slot_count, width, width)
        rights.append(densify(rp, recv_mr[step, 1, : groups * slot_count], RB, groups * RB))
        lefts.append(densify(recv_l[step], recv_ml[step, 0, :slot_count], RB, RB))
    square, overall = finish(lefts, rights, row_count, col_count, groups)
    trace_value = overall / math.sqrt(row_count * RB * width)
    return (square, trace_value)


def solution(mesh):
    return jax.shard_map(
        body,
        mesh=mesh,
        in_specs=(
            P("row", "col", None, None, None, None),
            P("row", "col", None, None),
            P("row", "col", None, None),
            P("row", "col", None),
        ),
        out_specs=(P("row", "col"), P()),
        check_vma=False,
    )
```

```python
import functools
import math

import jax
import jax.numpy as jnp
from jax import lax
from jax.experimental import pallas as pl
from jax.experimental.pallas import tpu as pltpu
from jax.sharding import PartitionSpec as P

RB = 5
STEPS = 4
MESH = pl.DeviceIdType.MESH


def densify(pieces, places, nrows, ncols):
    width = pieces.shape[-1]
    count = pieces.shape[0]
    onehot = (places[None, :] == jnp.arange(nrows * ncols, dtype=jnp.int32)[:, None]).astype(
        pieces.dtype
    )
    dense = jnp.dot(
        onehot, pieces.reshape(count, width * width), preferred_element_type=jnp.float32
    )
    dense = dense.reshape(nrows, ncols, width, width).transpose(0, 2, 1, 3)
    return dense.reshape(nrows * width, ncols * width).astype(pieces.dtype)


def exchange_kernel(row_count, col_count, groups,
                    blocks_ref, meta_ref, recv_l, recv_r, recv_ml, recv_mr, send_sem, recv_sem):
    r = lax.axis_index("row")
    c = lax.axis_index("col")
    a = r // groups
    b = r % groups

    def l_self(s):
        return (a + s) % col_count == 0

    def r_self(s):
        return (c + s) % col_count == 0

    def l_at(shift):
        return (r, (c + shift + 4 * col_count) % col_count)

    def r_at(shift):
        return ((r + shift + 4 * row_count) % row_count, c)

    left_plan, right_plan = {}, {}
    left_plan[1] = (l_self(1), l_at(-(a + 1)), l_at(a + 1))
    right_plan[1] = (r_self(1), r_at(-groups * (c + 1)), r_at(groups * (c + 1)))
    for s in (0, 2, 3):
        left_plan[s] = (l_self(s), l_at(1 - s), l_at(s - 1))
        right_plan[s] = (r_self(s), r_at(groups * (1 - s)), r_at(groups * (s - 1)))

    barrier = pltpu.get_barrier_semaphore()
    peers = 0
    for plan in (left_plan, right_plan):
        for s in range(STEPS):
            is_self, dst, src = plan[s]

            @pl.when(jnp.logical_not(is_self))
            def _(dst=dst, src=src):
                pl.semaphore_signal(barrier, 1, device_id=dst, device_id_type=MESH)
                pl.semaphore_signal(barrier, 1, device_id=src, device_id_type=MESH)

            peers = peers + jnp.where(is_self, 0, 2)
    pl.semaphore_wait(barrier, peers)

    sides = [
        (left_plan, meta_ref, lambda s: recv_ml.at[s]),
        (right_plan, meta_ref, lambda s: recv_mr.at[s]),
        (left_plan, blocks_ref.at[b], lambda s: recv_l.at[s]),
    ]
    for g in range(groups):
        sides.append((right_plan, blocks_ref.at[g], lambda s, g=g: recv_r.at[s, g]))
    kinds = len(sides)

    def transfer(plan, s, source, target, j):
        is_self, dst, _ = plan[s]
        k = kinds * s + j
        local = pltpu.make_async_copy(source, target, recv_sem.at[k])
        remote = pltpu.make_async_remote_copy(
            source, target, send_sem.at[k], recv_sem.at[k],
            device_id=dst, device_id_type=MESH,
        )
        return is_self, local, remote

    def finish_recv(job):
        is_self, local, remote = job

        @pl.when(is_self)
        def _():
            local.wait()

        @pl.when(jnp.logical_not(is_self))
        def _():
            remote.wait_recv()

    firsts = []
    for j, (plan, source, target) in enumerate(sides):
        job = transfer(plan, 1, source, target(1), j)
        firsts.append(job)
        is_self, local, remote = job

        @pl.when(is_self)
        def _(local=local):
            local.start()

        @pl.when(jnp.logical_not(is_self))
        def _(remote=remote):
            remote.start()

    for j, (plan, source, target) in enumerate(sides):
        for s in (0, 2, 3):
            is_self, local, remote = transfer(plan, s, source, target(s), j)

            @pl.when(is_self)
            def _(local=local):
                local.start()

    forwards = []
    for j, (plan, source, target) in enumerate(sides):
        finish_recv(firsts[j])
        for s in (0, 2, 3):
            job = transfer(plan, s, target(1), target(s), j)
            forwards.append(job)
            is_self, local, remote = job

            @pl.when(jnp.logical_not(is_self))
            def _(remote=remote):
                remote.start()

    for job in forwards:
        finish_recv(job)
    for is_self, local, remote in firsts + forwards:
        @pl.when(jnp.logical_not(is_self))
        def _(remote=remote):
            remote.wait_send()


def exchange(blocks, meta, row_count, col_count):
    groups, slots, width = blocks.shape[0], blocks.shape[1], blocks.shape[2]
    vmem = pl.BlockSpec(memory_space=pltpu.VMEM)
    return pl.pallas_call(
        functools.partial(exchange_kernel, row_count, col_count, groups),
        out_shape=(
            jax.ShapeDtypeStruct((STEPS, slots, width, width), blocks.dtype),
            jax.ShapeDtypeStruct((STEPS, groups, slots, width, width), blocks.dtype),
            jax.ShapeDtypeStruct((STEPS,) + meta.shape, meta.dtype),
            jax.ShapeDtypeStruct((STEPS,) + meta.shape, meta.dtype),
        ),
        in_specs=[vmem, vmem],
        out_specs=(vmem, vmem, vmem, vmem),
        scratch_shapes=[
            pltpu.SemaphoreType.DMA(((3 + groups) * STEPS,)),
            pltpu.SemaphoreType.DMA(((3 + groups) * STEPS,)),
        ],
        compiler_params=pltpu.CompilerParams(collective_id=0, has_side_effects=True),
    )(blocks, meta)


def trace_kernel(row_count, col_count, groups, scale_width,
                 term_ref, out_ref, row_buf, col_buf, send_sem, recv_sem, col_send, col_recv):
    r = lax.axis_index("row")
    c = lax.axis_index("col")
    diagonal = c == r // groups
    barrier = pltpu.get_barrier_semaphore()

    @pl.when(diagonal)
    def _():
        for cc in range(col_count):
            @pl.when(cc != c)
            def _(cc=cc):
                pl.semaphore_signal(barrier, 1, device_id=(r, cc), device_id_type=MESH)

    @pl.when(jnp.logical_not(diagonal))
    def _():
        pl.semaphore_signal(barrier, 1, device_id=(r, r // groups), device_id_type=MESH)

    for rr in range(row_count):
        @pl.when(rr != r)
        def _(rr=rr):
            pl.semaphore_signal(barrier, 1, device_id=(rr, c), device_id_type=MESH)

    pl.semaphore_wait(barrier, (row_count - 1) + jnp.where(diagonal, col_count - 1, 1))

    row_copies = []
    for cc in range(col_count):
        row_copies.append(pltpu.make_async_remote_copy(
            term_ref, row_buf, send_sem.at[cc], recv_sem.at[0],
            device_id=(r, cc), device_id_type=MESH,
        ))

    @pl.when(diagonal)
    def _():
        for cc in range(col_count):
            @pl.when(cc != c)
            def _(cc=cc):
                row_copies[cc].start()

    @pl.when(jnp.logical_not(diagonal))
    def _():
        row_copies[0].wait_recv()

    def col_copy(source, rr):
        return pltpu.make_async_remote_copy(
            source, col_buf.at[r], col_send.at[rr], col_recv.at[r],
            device_id=(rr, c), device_id_type=MESH,
        )

    for source, chosen in ((term_ref, diagonal), (row_buf, jnp.logical_not(diagonal))):
        @pl.when(chosen)
        def _(source=source):
            for rr in range(row_count):
                @pl.when(rr != r)
                def _(rr=rr):
                    col_copy(source, rr).start()

    for rr in range(row_count):
        @pl.when(rr != r)
        def _(rr=rr):
            pltpu.make_async_remote_copy(
                term_ref, col_buf.at[rr], col_send.at[rr], col_recv.at[rr],
                device_id=(rr, c), device_id_type=MESH,
            ).wait_recv()

    for source, chosen in ((term_ref, diagonal), (row_buf, jnp.logical_not(diagonal))):
        @pl.when(chosen)
        def _(source=source):
            for rr in range(row_count):
                @pl.when(rr != r)
                def _(rr=rr):
                    col_copy(source, rr).wait_send()
            col_buf[r] = source[...]

    @pl.when(diagonal)
    def _():
        for cc in range(col_count):
            @pl.when(cc != c)
            def _(cc=cc):
                row_copies[cc].wait_send()

    total = jnp.zeros(col_buf.shape[1:], jnp.float32)
    for rr in range(row_count):
        total = total + col_buf[rr]
    out_ref[...] = total[0:1, 0:1] / math.sqrt(row_count * RB * scale_width)


def trace_total(term, row_count, col_count, groups, width):
    tile = jnp.broadcast_to(term, (8, 128))
    vmem = pl.BlockSpec(memory_space=pltpu.VMEM)
    out = pl.pallas_call(
        functools.partial(trace_kernel, row_count, col_count, groups, width),
        out_shape=jax.ShapeDtypeStruct((1, 1), jnp.float32),
        in_specs=[vmem],
        out_specs=vmem,
        scratch_shapes=[
            pltpu.VMEM((8, 128), jnp.float32),
            pltpu.VMEM((row_count, 8, 128), jnp.float32),
            pltpu.SemaphoreType.DMA((col_count,)),
            pltpu.SemaphoreType.DMA((1,)),
            pltpu.SemaphoreType.DMA((row_count,)),
            pltpu.SemaphoreType.DMA((row_count,)),
        ],
        compiler_params=pltpu.CompilerParams(collective_id=1, has_side_effects=True),
    )(tile)
    return out.reshape(())


def body(blocks, block_rows, block_cols, counts):
    groups = blocks.shape[2]
    slot_count = blocks.shape[3]
    width = blocks.shape[4]
    row_count = lax.axis_size("row")
    col_count = lax.axis_size("col")
    row_place = lax.axis_index("row")
    col_place = lax.axis_index("col")
    lower = row_place % groups
    filled = counts[0, 0]
    live = jnp.arange(slot_count, dtype=jnp.int32)[None, :] < filled[:, None]
    left_places_all = jnp.where(live, block_rows[0, 0] * RB + block_cols[0, 0], -1)
    offsets = (jnp.arange(groups, dtype=jnp.int32) * RB)[:, None]
    right_places = jnp.where(
        live, block_rows[0, 0] * (groups * RB) + block_cols[0, 0] + offsets, -1
    ).reshape(-1)
    left_places = lax.dynamic_index_in_dim(left_places_all, lower, 0, keepdims=False)
    meta = jnp.zeros((8, 128), jnp.int32)
    meta = meta.at[0, :slot_count].set(left_places)
    meta = meta.at[1, : groups * slot_count].set(right_places)
    recv_l, recv_r, recv_ml, recv_mr = exchange(blocks[0, 0], meta, row_count, col_count)
    totals = jnp.zeros((RB * width, groups * RB * width), jnp.float32)
    for step in range(STEPS):
        rp = recv_r[step].reshape(groups * slot_count, width, width)
        right_dense = densify(rp, recv_mr[step, 1, : groups * slot_count], RB, groups * RB)
        left_dense = densify(recv_l[step], recv_ml[step, 0, :slot_count], RB, RB)
        totals = totals + jnp.dot(left_dense, right_dense, preferred_element_type=jnp.float32)
    shift_amount = row_place - groups * col_place
    valid = (shift_amount >= 0) & (shift_amount < groups)
    start = jnp.clip(shift_amount, 0, groups - 1) * RB * width
    window = lax.dynamic_slice_in_dim(totals, start, RB * width, 1)
    term = jnp.where(valid, jnp.trace(window), jnp.zeros((), jnp.float32))
    trace_value = trace_total(term, row_count, col_count, groups, width)
    return (totals.astype(jnp.bfloat16), trace_value)


def solution(mesh):
    return jax.shard_map(
        body,
        mesh=mesh,
        in_specs=(
            P("row", "col", None, None, None, None),
            P("row", "col", None, None),
            P("row", "col", None, None),
            P("row", "col", None),
        ),
        out_specs=(P("row", "col"), P()),
        check_vma=False,
    )
```

```python
import functools
import math

import jax
import jax.numpy as jnp
from jax import lax
from jax.experimental import pallas as pl
from jax.experimental.pallas import tpu as pltpu
from jax.sharding import PartitionSpec as P

RB = 5
STEPS = 4
MESH = pl.DeviceIdType.MESH


def densify(pieces, places, nrows, ncols):
    width = pieces.shape[-1]
    count = pieces.shape[0]
    onehot = (places[None, :] == jnp.arange(nrows * ncols, dtype=jnp.int32)[:, None]).astype(
        pieces.dtype
    )
    dense = jnp.dot(
        onehot, pieces.reshape(count, width * width), preferred_element_type=jnp.float32
    )
    dense = dense.reshape(nrows, ncols, width, width).transpose(0, 2, 1, 3)
    return dense.reshape(nrows * width, ncols * width).astype(pieces.dtype)


def exchange_kernel(row_count, col_count, groups,
                    blocks_ref, meta_ref, recv_l, recv_r, recv_ml, recv_mr, send_sem, recv_sem):
    r = lax.axis_index("row")
    c = lax.axis_index("col")
    a = r // groups
    b = r % groups

    def l_self(s):
        return (a + s) % col_count == 0

    def r_self(s):
        return (c + s) % col_count == 0

    def l_at(shift):
        return (r, (c + shift + 4 * col_count) % col_count)

    def r_at(shift):
        return ((r + shift + 4 * row_count) % row_count, c)

    left_plan, right_plan = {}, {}
    left_plan[1] = (l_self(1), l_at(-(a + 1)), l_at(a + 1))
    right_plan[1] = (r_self(1), r_at(-groups * (c + 1)), r_at(groups * (c + 1)))
    for s in (0, 2, 3):
        left_plan[s] = (l_self(s), l_at(1 - s), l_at(s - 1))
        right_plan[s] = (r_self(s), r_at(groups * (1 - s)), r_at(groups * (s - 1)))

    barrier = pltpu.get_barrier_semaphore()
    peers = 0
    for plan in (left_plan, right_plan):
        for s in range(STEPS):
            is_self, dst, src = plan[s]

            @pl.when(jnp.logical_not(is_self))
            def _(dst=dst, src=src):
                pl.semaphore_signal(barrier, 1, device_id=dst, device_id_type=MESH)
                pl.semaphore_signal(barrier, 1, device_id=src, device_id_type=MESH)

            peers = peers + jnp.where(is_self, 0, 2)
    pl.semaphore_wait(barrier, peers)

    sides = [
        (left_plan, meta_ref, lambda s: recv_ml.at[s]),
        (right_plan, meta_ref, lambda s: recv_mr.at[s]),
        (left_plan, blocks_ref.at[b], lambda s: recv_l.at[s]),
    ]
    for g in range(groups):
        sides.append((right_plan, blocks_ref.at[g], lambda s, g=g: recv_r.at[s, g]))
    kinds = len(sides)

    def transfer(plan, s, source, target, j):
        is_self, dst, _ = plan[s]
        k = kinds * s + j
        local = pltpu.make_async_copy(source, target, recv_sem.at[k])
        remote = pltpu.make_async_remote_copy(
            source, target, send_sem.at[k], recv_sem.at[k],
            device_id=dst, device_id_type=MESH,
        )
        return is_self, local, remote

    def finish_recv(job):
        is_self, local, remote = job

        @pl.when(is_self)
        def _():
            local.wait()

        @pl.when(jnp.logical_not(is_self))
        def _():
            remote.wait_recv()

    firsts = []
    for j, (plan, source, target) in enumerate(sides):
        job = transfer(plan, 1, source, target(1), j)
        firsts.append(job)
        is_self, local, remote = job

        @pl.when(is_self)
        def _(local=local):
            local.start()

        @pl.when(jnp.logical_not(is_self))
        def _(remote=remote):
            remote.start()

    for j, (plan, source, target) in enumerate(sides):
        for s in (0, 2, 3):
            is_self, local, remote = transfer(plan, s, source, target(s), j)

            @pl.when(is_self)
            def _(local=local):
                local.start()

    forwards = []
    for j, (plan, source, target) in enumerate(sides):
        finish_recv(firsts[j])
        for s in (0, 2, 3):
            job = transfer(plan, s, target(1), target(s), j)
            forwards.append(job)
            is_self, local, remote = job

            @pl.when(jnp.logical_not(is_self))
            def _(remote=remote):
                remote.start()

    for job in forwards:
        finish_recv(job)
    for is_self, local, remote in firsts + forwards:
        @pl.when(jnp.logical_not(is_self))
        def _(remote=remote):
            remote.wait_send()


def exchange(blocks, meta, row_count, col_count):
    groups, slots, width = blocks.shape[0], blocks.shape[1], blocks.shape[2]
    vmem = pl.BlockSpec(memory_space=pltpu.VMEM)
    return pl.pallas_call(
        functools.partial(exchange_kernel, row_count, col_count, groups),
        out_shape=(
            jax.ShapeDtypeStruct((STEPS, slots, width, width), blocks.dtype),
            jax.ShapeDtypeStruct((STEPS, groups, slots, width, width), blocks.dtype),
            jax.ShapeDtypeStruct((STEPS,) + meta.shape, meta.dtype),
            jax.ShapeDtypeStruct((STEPS,) + meta.shape, meta.dtype),
        ),
        in_specs=[vmem, vmem],
        out_specs=(vmem, vmem, vmem, vmem),
        scratch_shapes=[
            pltpu.SemaphoreType.DMA(((3 + groups) * STEPS,)),
            pltpu.SemaphoreType.DMA(((3 + groups) * STEPS,)),
        ],
        compiler_params=pltpu.CompilerParams(collective_id=0, has_side_effects=True),
    )(blocks, meta)


def trace_kernel(row_count, col_count, groups, scale_width,
                 term_ref, out_ref, row_buf, col_buf, send_sem, recv_sem, col_send, col_recv):
    r = lax.axis_index("row")
    c = lax.axis_index("col")
    diagonal = c == r // groups
    barrier = pltpu.get_barrier_semaphore()

    @pl.when(diagonal)
    def _():
        for cc in range(col_count):
            @pl.when(cc != c)
            def _(cc=cc):
                pl.semaphore_signal(barrier, 1, device_id=(r, cc), device_id_type=MESH)

    @pl.when(jnp.logical_not(diagonal))
    def _():
        pl.semaphore_signal(barrier, 1, device_id=(r, r // groups), device_id_type=MESH)

    for rr in range(row_count):
        @pl.when(rr != r)
        def _(rr=rr):
            pl.semaphore_signal(barrier, 1, device_id=(rr, c), device_id_type=MESH)

    pl.semaphore_wait(barrier, (row_count - 1) + jnp.where(diagonal, col_count - 1, 1))

    row_copies = []
    for cc in range(col_count):
        row_copies.append(pltpu.make_async_remote_copy(
            term_ref, row_buf, send_sem.at[cc], recv_sem.at[0],
            device_id=(r, cc), device_id_type=MESH,
        ))

    @pl.when(diagonal)
    def _():
        for cc in range(col_count):
            @pl.when(cc != c)
            def _(cc=cc):
                row_copies[cc].start()

    @pl.when(jnp.logical_not(diagonal))
    def _():
        row_copies[0].wait_recv()

    def col_copy(source, rr):
        return pltpu.make_async_remote_copy(
            source, col_buf.at[r], col_send.at[rr], col_recv.at[r],
            device_id=(rr, c), device_id_type=MESH,
        )

    for source, chosen in ((term_ref, diagonal), (row_buf, jnp.logical_not(diagonal))):
        @pl.when(chosen)
        def _(source=source):
            for rr in range(row_count):
                @pl.when(rr != r)
                def _(rr=rr):
                    col_copy(source, rr).start()

    for rr in range(row_count):
        @pl.when(rr != r)
        def _(rr=rr):
            pltpu.make_async_remote_copy(
                term_ref, col_buf.at[rr], col_send.at[rr], col_recv.at[rr],
                device_id=(rr, c), device_id_type=MESH,
            ).wait_recv()

    for source, chosen in ((term_ref, diagonal), (row_buf, jnp.logical_not(diagonal))):
        @pl.when(chosen)
        def _(source=source):
            for rr in range(row_count):
                @pl.when(rr != r)
                def _(rr=rr):
                    col_copy(source, rr).wait_send()
            col_buf[r] = source[...]

    @pl.when(diagonal)
    def _():
        for cc in range(col_count):
            @pl.when(cc != c)
            def _(cc=cc):
                row_copies[cc].wait_send()

    total = jnp.zeros(col_buf.shape[1:], jnp.float32)
    for rr in range(row_count):
        total = total + col_buf[rr]
    out_ref[...] = total[0:1, 0:1] / math.sqrt(row_count * RB * scale_width)


def trace_total(term, row_count, col_count, groups, width):
    tile = term.reshape(1, 1)
    vmem = pl.BlockSpec(memory_space=pltpu.VMEM)
    out = pl.pallas_call(
        functools.partial(trace_kernel, row_count, col_count, groups, width),
        out_shape=jax.ShapeDtypeStruct((1, 1), jnp.float32),
        in_specs=[vmem],
        out_specs=vmem,
        scratch_shapes=[
            pltpu.VMEM((1, 1), jnp.float32),
            pltpu.VMEM((row_count, 1, 1), jnp.float32),
            pltpu.SemaphoreType.DMA((col_count,)),
            pltpu.SemaphoreType.DMA((1,)),
            pltpu.SemaphoreType.DMA((row_count,)),
            pltpu.SemaphoreType.DMA((row_count,)),
        ],
        compiler_params=pltpu.CompilerParams(collective_id=1, has_side_effects=True),
    )(tile)
    return out.reshape(())


def body(blocks, block_rows, block_cols, counts):
    groups = blocks.shape[2]
    slot_count = blocks.shape[3]
    width = blocks.shape[4]
    row_count = lax.axis_size("row")
    col_count = lax.axis_size("col")
    row_place = lax.axis_index("row")
    col_place = lax.axis_index("col")
    lower = row_place % groups
    filled = counts[0, 0]
    live = jnp.arange(slot_count, dtype=jnp.int32)[None, :] < filled[:, None]
    left_places_all = jnp.where(live, block_rows[0, 0] * RB + block_cols[0, 0], -1)
    offsets = (jnp.arange(groups, dtype=jnp.int32) * RB)[:, None]
    right_places = jnp.where(
        live, block_rows[0, 0] * (groups * RB) + block_cols[0, 0] + offsets, -1
    ).reshape(-1)
    left_places = lax.dynamic_index_in_dim(left_places_all, lower, 0, keepdims=False)
    meta = jnp.zeros((8, 128), jnp.int32)
    meta = meta.at[0, :slot_count].set(left_places)
    meta = meta.at[1, : groups * slot_count].set(right_places)
    recv_l, recv_r, recv_ml, recv_mr = exchange(blocks[0, 0], meta, row_count, col_count)
    totals = jnp.zeros((RB * width, groups * RB * width), jnp.float32)
    for step in range(STEPS):
        rp = recv_r[step].reshape(groups * slot_count, width, width)
        right_dense = densify(rp, recv_mr[step, 1, : groups * slot_count], RB, groups * RB)
        left_dense = densify(recv_l[step], recv_ml[step, 0, :slot_count], RB, RB)
        totals = totals + jnp.dot(left_dense, right_dense, preferred_element_type=jnp.float32)
    shift_amount = row_place - groups * col_place
    valid = (shift_amount >= 0) & (shift_amount < groups)
    start = jnp.clip(shift_amount, 0, groups - 1) * RB * width
    window = lax.dynamic_slice_in_dim(totals, start, RB * width, 1)
    term = jnp.where(valid, jnp.trace(window), jnp.zeros((), jnp.float32))
    trace_value = trace_total(term, row_count, col_count, groups, width)
    return (totals.astype(jnp.bfloat16), trace_value)


def solution(mesh):
    return jax.shard_map(
        body,
        mesh=mesh,
        in_specs=(
            P("row", "col", None, None, None, None),
            P("row", "col", None, None),
            P("row", "col", None, None),
            P("row", "col", None),
        ),
        out_specs=(P("row", "col"), P()),
        check_vma=False,
    )
```

```python
import functools
import math

import jax
import jax.numpy as jnp
from jax import lax
from jax.experimental import pallas as pl
from jax.experimental.pallas import tpu as pltpu
from jax.sharding import PartitionSpec as P

RB = 5
STEPS = 4
MESH = pl.DeviceIdType.MESH


def densify(pieces, places, nrows, ncols):
    width = pieces.shape[-1]
    count = pieces.shape[0]
    onehot = (places[None, :] == jnp.arange(nrows * ncols, dtype=jnp.int32)[:, None]).astype(
        pieces.dtype
    )
    dense = jnp.dot(
        onehot, pieces.reshape(count, width * width), preferred_element_type=jnp.float32
    )
    dense = dense.reshape(nrows, ncols, width, width).transpose(0, 2, 1, 3)
    return dense.reshape(nrows * width, ncols * width).astype(pieces.dtype)


def exchange_kernel(row_count, col_count, groups,
                    blocks_ref, meta_ref, recv_l, recv_r, recv_ml, recv_mr, send_sem, recv_sem):
    r = lax.axis_index("row")
    c = lax.axis_index("col")
    a = r // groups
    b = r % groups

    def l_self(s):
        return (a + s) % col_count == 0

    def r_self(s):
        return (c + s) % col_count == 0

    def l_at(shift):
        return (r, (c + shift + 4 * col_count) % col_count)

    def r_at(shift):
        return ((r + shift + 4 * row_count) % row_count, c)

    left_plan, right_plan = {}, {}
    left_plan[1] = (l_self(1), l_at(-(a + 1)), l_at(a + 1))
    right_plan[1] = (r_self(1), r_at(-groups * (c + 1)), r_at(groups * (c + 1)))
    for s in (0, 2, 3):
        left_plan[s] = (l_self(s), l_at(1 - s), l_at(s - 1))
        right_plan[s] = (r_self(s), r_at(groups * (1 - s)), r_at(groups * (s - 1)))

    barrier = pltpu.get_barrier_semaphore()
    peers = 0
    for plan in (left_plan, right_plan):
        for s in range(STEPS):
            is_self, dst, src = plan[s]

            @pl.when(jnp.logical_not(is_self))
            def _(dst=dst, src=src):
                pl.semaphore_signal(barrier, 1, device_id=dst, device_id_type=MESH)
                pl.semaphore_signal(barrier, 1, device_id=src, device_id_type=MESH)

            peers = peers + jnp.where(is_self, 0, 2)
    pl.semaphore_wait(barrier, peers)

    sides = [
        (left_plan, meta_ref, lambda s: recv_ml.at[s]),
        (right_plan, meta_ref, lambda s: recv_mr.at[s]),
        (left_plan, blocks_ref.at[b], lambda s: recv_l.at[s]),
    ]
    for g in range(groups):
        sides.append((right_plan, blocks_ref.at[g], lambda s, g=g: recv_r.at[s, g]))
    kinds = len(sides)

    def transfer(plan, s, source, target, j):
        is_self, dst, _ = plan[s]
        k = kinds * s + j
        local = pltpu.make_async_copy(source, target, recv_sem.at[k])
        remote = pltpu.make_async_remote_copy(
            source, target, send_sem.at[k], recv_sem.at[k],
            device_id=dst, device_id_type=MESH,
        )
        return is_self, local, remote

    def finish_recv(job):
        is_self, local, remote = job

        @pl.when(is_self)
        def _():
            local.wait()

        @pl.when(jnp.logical_not(is_self))
        def _():
            remote.wait_recv()

    firsts = []
    for j, (plan, source, target) in enumerate(sides):
        job = transfer(plan, 1, source, target(1), j)
        firsts.append(job)
        is_self, local, remote = job

        @pl.when(is_self)
        def _(local=local):
            local.start()

        @pl.when(jnp.logical_not(is_self))
        def _(remote=remote):
            remote.start()

    for j, (plan, source, target) in enumerate(sides):
        for s in (0, 2, 3):
            is_self, local, remote = transfer(plan, s, source, target(s), j)

            @pl.when(is_self)
            def _(local=local):
                local.start()

    forwards = []
    for j, (plan, source, target) in enumerate(sides):
        finish_recv(firsts[j])
        for s in (0, 2, 3):
            job = transfer(plan, s, target(1), target(s), j)
            forwards.append(job)
            is_self, local, remote = job

            @pl.when(jnp.logical_not(is_self))
            def _(remote=remote):
                remote.start()

    for job in forwards:
        finish_recv(job)
    for is_self, local, remote in firsts + forwards:
        @pl.when(jnp.logical_not(is_self))
        def _(remote=remote):
            remote.wait_send()


def exchange(blocks, meta, row_count, col_count):
    groups, slots, width = blocks.shape[0], blocks.shape[1], blocks.shape[2]
    vmem = pl.BlockSpec(memory_space=pltpu.VMEM)
    return pl.pallas_call(
        functools.partial(exchange_kernel, row_count, col_count, groups),
        out_shape=(
            jax.ShapeDtypeStruct((STEPS, slots, width, width), blocks.dtype),
            jax.ShapeDtypeStruct((STEPS, groups, slots, width, width), blocks.dtype),
            jax.ShapeDtypeStruct((STEPS,) + meta.shape, meta.dtype),
            jax.ShapeDtypeStruct((STEPS,) + meta.shape, meta.dtype),
        ),
        in_specs=[pl.BlockSpec(memory_space=pl.ANY), vmem],
        out_specs=(vmem, vmem, vmem, vmem),
        scratch_shapes=[
            pltpu.SemaphoreType.DMA(((3 + groups) * STEPS,)),
            pltpu.SemaphoreType.DMA(((3 + groups) * STEPS,)),
        ],
        compiler_params=pltpu.CompilerParams(collective_id=0, has_side_effects=True),
    )(blocks, meta)


def trace_kernel(row_count, col_count, groups, scale_width,
                 term_ref, out_ref, row_buf, col_buf, send_sem, recv_sem, col_send, col_recv):
    r = lax.axis_index("row")
    c = lax.axis_index("col")
    diagonal = c == r // groups
    barrier = pltpu.get_barrier_semaphore()

    @pl.when(diagonal)
    def _():
        for cc in range(col_count):
            @pl.when(cc != c)
            def _(cc=cc):
                pl.semaphore_signal(barrier, 1, device_id=(r, cc), device_id_type=MESH)

    @pl.when(jnp.logical_not(diagonal))
    def _():
        pl.semaphore_signal(barrier, 1, device_id=(r, r // groups), device_id_type=MESH)

    for rr in range(row_count):
        @pl.when(rr != r)
        def _(rr=rr):
            pl.semaphore_signal(barrier, 1, device_id=(rr, c), device_id_type=MESH)

    pl.semaphore_wait(barrier, (row_count - 1) + jnp.where(diagonal, col_count - 1, 1))

    row_copies = []
    for cc in range(col_count):
        row_copies.append(pltpu.make_async_remote_copy(
            term_ref, row_buf, send_sem.at[cc], recv_sem.at[0],
            device_id=(r, cc), device_id_type=MESH,
        ))

    @pl.when(diagonal)
    def _():
        for cc in range(col_count):
            @pl.when(cc != c)
            def _(cc=cc):
                row_copies[cc].start()

    @pl.when(jnp.logical_not(diagonal))
    def _():
        row_copies[0].wait_recv()

    def col_copy(source, rr):
        return pltpu.make_async_remote_copy(
            source, col_buf.at[r], col_send.at[rr], col_recv.at[r],
            device_id=(rr, c), device_id_type=MESH,
        )

    for source, chosen in ((term_ref, diagonal), (row_buf, jnp.logical_not(diagonal))):
        @pl.when(chosen)
        def _(source=source):
            for rr in range(row_count):
                @pl.when(rr != r)
                def _(rr=rr):
                    col_copy(source, rr).start()

    for rr in range(row_count):
        @pl.when(rr != r)
        def _(rr=rr):
            pltpu.make_async_remote_copy(
                term_ref, col_buf.at[rr], col_send.at[rr], col_recv.at[rr],
                device_id=(rr, c), device_id_type=MESH,
            ).wait_recv()

    for source, chosen in ((term_ref, diagonal), (row_buf, jnp.logical_not(diagonal))):
        @pl.when(chosen)
        def _(source=source):
            for rr in range(row_count):
                @pl.when(rr != r)
                def _(rr=rr):
                    col_copy(source, rr).wait_send()
            col_buf[r] = source[...]

    @pl.when(diagonal)
    def _():
        for cc in range(col_count):
            @pl.when(cc != c)
            def _(cc=cc):
                row_copies[cc].wait_send()

    total = jnp.zeros(col_buf.shape[1:], jnp.float32)
    for rr in range(row_count):
        total = total + col_buf[rr]
    out_ref[...] = total[0:1, 0:1] / math.sqrt(row_count * RB * scale_width)


def trace_total(term, row_count, col_count, groups, width):
    tile = term.reshape(1, 1)
    vmem = pl.BlockSpec(memory_space=pltpu.VMEM)
    out = pl.pallas_call(
        functools.partial(trace_kernel, row_count, col_count, groups, width),
        out_shape=jax.ShapeDtypeStruct((1, 1), jnp.float32),
        in_specs=[vmem],
        out_specs=vmem,
        scratch_shapes=[
            pltpu.VMEM((1, 1), jnp.float32),
            pltpu.VMEM((row_count, 1, 1), jnp.float32),
            pltpu.SemaphoreType.DMA((col_count,)),
            pltpu.SemaphoreType.DMA((1,)),
            pltpu.SemaphoreType.DMA((row_count,)),
            pltpu.SemaphoreType.DMA((row_count,)),
        ],
        compiler_params=pltpu.CompilerParams(collective_id=1, has_side_effects=True),
    )(tile)
    return out.reshape(())


def body(blocks, block_rows, block_cols, counts):
    groups = blocks.shape[2]
    slot_count = blocks.shape[3]
    width = blocks.shape[4]
    row_count = lax.axis_size("row")
    col_count = lax.axis_size("col")
    row_place = lax.axis_index("row")
    col_place = lax.axis_index("col")
    lower = row_place % groups
    filled = counts[0, 0]
    live = jnp.arange(slot_count, dtype=jnp.int32)[None, :] < filled[:, None]
    left_places_all = jnp.where(live, block_rows[0, 0] * RB + block_cols[0, 0], -1)
    offsets = (jnp.arange(groups, dtype=jnp.int32) * RB)[:, None]
    right_places = jnp.where(
        live, block_rows[0, 0] * (groups * RB) + block_cols[0, 0] + offsets, -1
    ).reshape(-1)
    left_places = lax.dynamic_index_in_dim(left_places_all, lower, 0, keepdims=False)
    meta = jnp.stack([
        jnp.pad(left_places, (0, 128 - slot_count)),
        jnp.pad(right_places, (0, 128 - groups * slot_count)),
    ])
    meta = jnp.pad(meta, ((0, 6), (0, 0)))
    recv_l, recv_r, recv_ml, recv_mr = exchange(blocks[0, 0], meta, row_count, col_count)
    totals = jnp.zeros((RB * width, groups * RB * width), jnp.float32)
    for step in range(STEPS):
        rp = recv_r[step].reshape(groups * slot_count, width, width)
        right_dense = densify(rp, recv_mr[step, 1, : groups * slot_count], RB, groups * RB)
        left_dense = densify(recv_l[step], recv_ml[step, 0, :slot_count], RB, RB)
        totals = totals + jnp.dot(left_dense, right_dense, preferred_element_type=jnp.float32)
    shift_amount = row_place - groups * col_place
    valid = (shift_amount >= 0) & (shift_amount < groups)
    start = jnp.clip(shift_amount, 0, groups - 1) * RB * width
    window = lax.dynamic_slice_in_dim(totals, start, RB * width, 1)
    term = jnp.where(valid, jnp.trace(window), jnp.zeros((), jnp.float32))
    trace_value = trace_total(term, row_count, col_count, groups, width)
    return (totals.astype(jnp.bfloat16), trace_value)


def solution(mesh):
    return jax.shard_map(
        body,
        mesh=mesh,
        in_specs=(
            P("row", "col", None, None, None, None),
            P("row", "col", None, None),
            P("row", "col", None, None),
            P("row", "col", None),
        ),
        out_specs=(P("row", "col"), P()),
        check_vma=False,
    )
```

```python
import functools
import math

import jax
import jax.numpy as jnp
from jax import lax
from jax.experimental import pallas as pl
from jax.experimental.pallas import tpu as pltpu
from jax.sharding import PartitionSpec as P

RB = 5
STEPS = 4
MESH = pl.DeviceIdType.MESH


def densify(pieces, places, nrows, ncols):
    width = pieces.shape[-1]
    count = pieces.shape[0]
    onehot = (places[None, :] == jnp.arange(nrows * ncols, dtype=jnp.int32)[:, None]).astype(
        pieces.dtype
    )
    dense = jnp.dot(
        onehot, pieces.reshape(count, width * width), preferred_element_type=jnp.float32
    )
    dense = dense.reshape(nrows, ncols, width, width).transpose(0, 2, 1, 3)
    return dense.reshape(nrows * width, ncols * width).astype(pieces.dtype)


def exchange_kernel(row_count, col_count, groups,
                    blocks_ref, meta_ref, recv_l, recv_r, recv_ml, recv_mr, send_sem, recv_sem):
    r = lax.axis_index("row")
    c = lax.axis_index("col")
    a = r // groups
    b = r % groups

    def l_self(s):
        return (a + s) % col_count == 0

    def r_self(s):
        return (c + s) % col_count == 0

    def l_at(shift):
        return (r, (c + shift + 4 * col_count) % col_count)

    def r_at(shift):
        return ((r + shift + 4 * row_count) % row_count, c)

    left_plan, right_plan = {}, {}
    left_plan[1] = (l_self(1), l_at(-(a + 1)), l_at(a + 1))
    right_plan[1] = (r_self(1), r_at(-groups * (c + 1)), r_at(groups * (c + 1)))
    for s in (0, 2, 3):
        left_plan[s] = (l_self(s), l_at(1 - s), l_at(s - 1))
        right_plan[s] = (r_self(s), r_at(groups * (1 - s)), r_at(groups * (s - 1)))

    barrier = pltpu.get_barrier_semaphore()
    peers = 0
    for plan in (left_plan, right_plan):
        for s in range(STEPS):
            is_self, dst, src = plan[s]

            @pl.when(jnp.logical_not(is_self))
            def _(dst=dst, src=src):
                pl.semaphore_signal(barrier, 1, device_id=dst, device_id_type=MESH)
                pl.semaphore_signal(barrier, 1, device_id=src, device_id_type=MESH)

            peers = peers + jnp.where(is_self, 0, 2)
    pl.semaphore_wait(barrier, peers)

    sides = [
        (left_plan, meta_ref, lambda s: recv_ml.at[s]),
        (right_plan, meta_ref, lambda s: recv_mr.at[s]),
        (left_plan, blocks_ref.at[b], lambda s: recv_l.at[s]),
    ]
    for g in range(groups):
        sides.append((right_plan, blocks_ref.at[g], lambda s, g=g: recv_r.at[s, g]))
    kinds = len(sides)

    def transfer(plan, s, source, target, j):
        is_self, dst, _ = plan[s]
        k = kinds * s + j
        local = pltpu.make_async_copy(source, target, recv_sem.at[k])
        remote = pltpu.make_async_remote_copy(
            source, target, send_sem.at[k], recv_sem.at[k],
            device_id=dst, device_id_type=MESH,
        )
        return is_self, local, remote

    def finish_recv(job):
        is_self, local, remote = job

        @pl.when(is_self)
        def _():
            local.wait()

        @pl.when(jnp.logical_not(is_self))
        def _():
            remote.wait_recv()

    firsts = []
    for j, (plan, source, target) in enumerate(sides):
        job = transfer(plan, 1, source, target(1), j)
        firsts.append(job)
        is_self, local, remote = job

        @pl.when(is_self)
        def _(local=local):
            local.start()

        @pl.when(jnp.logical_not(is_self))
        def _(remote=remote):
            remote.start()

    for j, (plan, source, target) in enumerate(sides):
        for s in (0, 2, 3):
            is_self, local, remote = transfer(plan, s, source, target(s), j)

            @pl.when(is_self)
            def _(local=local):
                local.start()

    forwards = []
    for j, (plan, source, target) in enumerate(sides):
        finish_recv(firsts[j])
        for s in (0, 2, 3):
            job = transfer(plan, s, target(1), target(s), j)
            forwards.append(job)
            is_self, local, remote = job

            @pl.when(jnp.logical_not(is_self))
            def _(remote=remote):
                remote.start()

    for job in forwards:
        finish_recv(job)
    for is_self, local, remote in firsts + forwards:
        @pl.when(jnp.logical_not(is_self))
        def _(remote=remote):
            remote.wait_send()


def exchange(blocks, meta, row_count, col_count):
    groups, slots, width = blocks.shape[0], blocks.shape[1], blocks.shape[2]
    vmem = pl.BlockSpec(memory_space=pltpu.VMEM)
    return pl.pallas_call(
        functools.partial(exchange_kernel, row_count, col_count, groups),
        out_shape=(
            jax.ShapeDtypeStruct((STEPS, slots, width, width), blocks.dtype),
            jax.ShapeDtypeStruct((STEPS, groups, slots, width, width), blocks.dtype),
            jax.ShapeDtypeStruct((STEPS,) + meta.shape, meta.dtype),
            jax.ShapeDtypeStruct((STEPS,) + meta.shape, meta.dtype),
        ),
        in_specs=[pl.BlockSpec(memory_space=pl.ANY), vmem],
        out_specs=(vmem, vmem, vmem, vmem),
        scratch_shapes=[
            pltpu.SemaphoreType.DMA(((3 + groups) * STEPS,)),
            pltpu.SemaphoreType.DMA(((3 + groups) * STEPS,)),
        ],
        compiler_params=pltpu.CompilerParams(collective_id=0, has_side_effects=True),
    )(blocks, meta)


def trace_kernel(row_count, col_count, groups, scale_width,
                 term_ref, out_ref, row_buf, col_buf, send_sem, recv_sem, col_send, col_recv):
    r = lax.axis_index("row")
    c = lax.axis_index("col")
    diagonal = c == r // groups
    barrier = pltpu.get_barrier_semaphore()

    @pl.when(diagonal)
    def _():
        for cc in range(col_count):
            @pl.when(cc != c)
            def _(cc=cc):
                pl.semaphore_signal(barrier, 1, device_id=(r, cc), device_id_type=MESH)

    @pl.when(jnp.logical_not(diagonal))
    def _():
        pl.semaphore_signal(barrier, 1, device_id=(r, r // groups), device_id_type=MESH)

    for rr in range(row_count):
        @pl.when(rr != r)
        def _(rr=rr):
            pl.semaphore_signal(barrier, 1, device_id=(rr, c), device_id_type=MESH)

    pl.semaphore_wait(barrier, (row_count - 1) + jnp.where(diagonal, col_count - 1, 1))

    row_copies = []
    for cc in range(col_count):
        row_copies.append(pltpu.make_async_remote_copy(
            term_ref, row_buf, send_sem.at[cc], recv_sem.at[0],
            device_id=(r, cc), device_id_type=MESH,
        ))

    @pl.when(diagonal)
    def _():
        for cc in range(col_count):
            @pl.when(cc != c)
            def _(cc=cc):
                row_copies[cc].start()

    @pl.when(jnp.logical_not(diagonal))
    def _():
        row_copies[0].wait_recv()

    def col_copy(source, rr):
        return pltpu.make_async_remote_copy(
            source, col_buf.at[r], col_send.at[rr], col_recv.at[r],
            device_id=(rr, c), device_id_type=MESH,
        )

    for source, chosen in ((term_ref, diagonal), (row_buf, jnp.logical_not(diagonal))):
        @pl.when(chosen)
        def _(source=source):
            for rr in range(row_count):
                @pl.when(rr != r)
                def _(rr=rr):
                    col_copy(source, rr).start()

    for rr in range(row_count):
        @pl.when(rr != r)
        def _(rr=rr):
            pltpu.make_async_remote_copy(
                term_ref, col_buf.at[rr], col_send.at[rr], col_recv.at[rr],
                device_id=(rr, c), device_id_type=MESH,
            ).wait_recv()

    for source, chosen in ((term_ref, diagonal), (row_buf, jnp.logical_not(diagonal))):
        @pl.when(chosen)
        def _(source=source):
            for rr in range(row_count):
                @pl.when(rr != r)
                def _(rr=rr):
                    col_copy(source, rr).wait_send()
            col_buf[r] = source[...]

    @pl.when(diagonal)
    def _():
        for cc in range(col_count):
            @pl.when(cc != c)
            def _(cc=cc):
                row_copies[cc].wait_send()

    total = jnp.zeros(col_buf.shape[1:], jnp.float32)
    for rr in range(row_count):
        total = total + col_buf[rr]
    out_ref[...] = total[0:1, 0:1] / math.sqrt(row_count * RB * scale_width)


def trace_total(term, row_count, col_count, groups, width):
    tile = term.reshape(1, 1)
    vmem = pl.BlockSpec(memory_space=pltpu.VMEM)
    out = pl.pallas_call(
        functools.partial(trace_kernel, row_count, col_count, groups, width),
        out_shape=jax.ShapeDtypeStruct((1, 1), jnp.float32),
        in_specs=[vmem],
        out_specs=vmem,
        scratch_shapes=[
            pltpu.VMEM((1, 1), jnp.float32),
            pltpu.VMEM((row_count, 1, 1), jnp.float32),
            pltpu.SemaphoreType.DMA((col_count,)),
            pltpu.SemaphoreType.DMA((1,)),
            pltpu.SemaphoreType.DMA((row_count,)),
            pltpu.SemaphoreType.DMA((row_count,)),
        ],
        compiler_params=pltpu.CompilerParams(collective_id=1, has_side_effects=True),
    )(tile)
    return out.reshape(())


def body(blocks, block_rows, block_cols, counts):
    groups = blocks.shape[2]
    slot_count = blocks.shape[3]
    width = blocks.shape[4]
    row_count = lax.axis_size("row")
    col_count = lax.axis_size("col")
    row_place = lax.axis_index("row")
    col_place = lax.axis_index("col")
    lower = row_place % groups
    filled = counts[0, 0]
    live = jnp.arange(slot_count, dtype=jnp.int32)[None, :] < filled[:, None]
    left_places_all = jnp.where(live, block_rows[0, 0] * RB + block_cols[0, 0], -1)
    offsets = (jnp.arange(groups, dtype=jnp.int32) * RB)[:, None]
    right_places = jnp.where(
        live, block_rows[0, 0] * (groups * RB) + block_cols[0, 0] + offsets, -1
    ).reshape(-1)
    left_places = lax.dynamic_index_in_dim(left_places_all, lower, 0, keepdims=False)
    meta = jnp.stack([
        jnp.pad(left_places, (0, 128 - slot_count)),
        jnp.pad(right_places, (0, 128 - groups * slot_count)),
    ])
    recv_l, recv_r, recv_ml, recv_mr = exchange(blocks[0, 0], meta, row_count, col_count)
    totals = jnp.zeros((RB * width, groups * RB * width), jnp.float32)
    for step in range(STEPS):
        rp = recv_r[step].reshape(groups * slot_count, width, width)
        right_dense = densify(rp, recv_mr[step, 1, : groups * slot_count], RB, groups * RB)
        left_dense = densify(recv_l[step], recv_ml[step, 0, :slot_count], RB, RB)
        totals = totals + jnp.dot(left_dense, right_dense, preferred_element_type=jnp.float32)
    shift_amount = row_place - groups * col_place
    valid = (shift_amount >= 0) & (shift_amount < groups)
    start = jnp.clip(shift_amount, 0, groups - 1) * RB * width
    window = lax.dynamic_slice_in_dim(totals, start, RB * width, 1)
    term = jnp.where(valid, jnp.trace(window), jnp.zeros((), jnp.float32))
    trace_value = trace_total(term, row_count, col_count, groups, width)
    return (totals.astype(jnp.bfloat16), trace_value)


def solution(mesh):
    return jax.shard_map(
        body,
        mesh=mesh,
        in_specs=(
            P("row", "col", None, None, None, None),
            P("row", "col", None, None),
            P("row", "col", None, None),
            P("row", "col", None),
        ),
        out_specs=(P("row", "col"), P()),
        check_vma=False,
    )
```

```python
import functools
import math

import jax
import jax.numpy as jnp
from jax import lax
from jax.experimental import pallas as pl
from jax.experimental.pallas import tpu as pltpu
from jax.sharding import PartitionSpec as P

RB = 5
STEPS = 4
MESH = pl.DeviceIdType.MESH


def densify(pieces, places, nrows, ncols):
    width = pieces.shape[-1]
    count = pieces.shape[0]
    onehot = (places[None, :] == jnp.arange(nrows * ncols, dtype=jnp.int32)[:, None]).astype(
        pieces.dtype
    )
    dense = jnp.dot(
        onehot, pieces.reshape(count, width * width), preferred_element_type=jnp.float32
    )
    dense = dense.reshape(nrows, ncols, width, width).transpose(0, 2, 1, 3)
    return dense.reshape(nrows * width, ncols * width).astype(pieces.dtype)


def exchange_kernel(row_count, col_count, groups,
                    blocks_ref, meta_ref, recv_l, recv_r, recv_ml, recv_mr, send_sem, recv_sem):
    r = lax.axis_index("row")
    c = lax.axis_index("col")
    a = r // groups
    b = r % groups

    def l_self(s):
        return (a + s) % col_count == 0

    def r_self(s):
        return (c + s) % col_count == 0

    def l_at(shift):
        return (r, (c + shift + 4 * col_count) % col_count)

    def r_at(shift):
        return ((r + shift + 4 * row_count) % row_count, c)

    left_plan, right_plan = {}, {}
    left_plan[1] = (l_self(1), l_at(-(a + 1)), l_at(a + 1))
    right_plan[1] = (r_self(1), r_at(-groups * (c + 1)), r_at(groups * (c + 1)))
    for s in (0, 2, 3):
        left_plan[s] = (l_self(s), l_at(1 - s), l_at(s - 1))
        right_plan[s] = (r_self(s), r_at(groups * (1 - s)), r_at(groups * (s - 1)))

    barrier = pltpu.get_barrier_semaphore()
    peers = 0
    for plan in (left_plan, right_plan):
        for s in range(STEPS):
            is_self, dst, src = plan[s]

            @pl.when(jnp.logical_not(is_self))
            def _(dst=dst, src=src):
                pl.semaphore_signal(barrier, 1, device_id=dst, device_id_type=MESH)
                pl.semaphore_signal(barrier, 1, device_id=src, device_id_type=MESH)

            peers = peers + jnp.where(is_self, 0, 2)
    pl.semaphore_wait(barrier, peers)

    sides = [
        (left_plan, meta_ref, lambda s: recv_ml.at[s]),
        (right_plan, meta_ref, lambda s: recv_mr.at[s]),
        (left_plan, blocks_ref.at[b], lambda s: recv_l.at[s]),
    ]
    for g in range(groups):
        sides.append((right_plan, blocks_ref.at[g], lambda s, g=g: recv_r.at[s, g]))
    kinds = len(sides)

    def transfer(plan, s, source, target, j):
        is_self, dst, _ = plan[s]
        k = kinds * s + j
        local = pltpu.make_async_copy(source, target, recv_sem.at[k])
        remote = pltpu.make_async_remote_copy(
            source, target, send_sem.at[k], recv_sem.at[k],
            device_id=dst, device_id_type=MESH,
        )
        return is_self, local, remote

    def finish_recv(job):
        is_self, local, remote = job

        @pl.when(is_self)
        def _():
            local.wait()

        @pl.when(jnp.logical_not(is_self))
        def _():
            remote.wait_recv()

    firsts = []
    for j, (plan, source, target) in enumerate(sides):
        job = transfer(plan, 1, source, target(1), j)
        firsts.append(job)
        is_self, local, remote = job

        @pl.when(is_self)
        def _(local=local):
            local.start()

        @pl.when(jnp.logical_not(is_self))
        def _(remote=remote):
            remote.start()

    for j, (plan, source, target) in enumerate(sides):
        for s in (0, 2, 3):
            is_self, local, remote = transfer(plan, s, source, target(s), j)

            @pl.when(is_self)
            def _(local=local):
                local.start()

    forwards = []
    for j, (plan, source, target) in enumerate(sides):
        finish_recv(firsts[j])
        for s in (0, 2, 3):
            job = transfer(plan, s, target(1), target(s), j)
            forwards.append(job)
            is_self, local, remote = job

            @pl.when(jnp.logical_not(is_self))
            def _(remote=remote):
                remote.start()

    for job in forwards:
        finish_recv(job)
    for is_self, local, remote in firsts + forwards:
        @pl.when(jnp.logical_not(is_self))
        def _(remote=remote):
            remote.wait_send()


def exchange(blocks, meta, row_count, col_count):
    groups, slots, width = blocks.shape[0], blocks.shape[1], blocks.shape[2]
    vmem = pl.BlockSpec(memory_space=pltpu.VMEM)
    return pl.pallas_call(
        functools.partial(exchange_kernel, row_count, col_count, groups),
        out_shape=(
            jax.ShapeDtypeStruct((STEPS, slots, width, width), blocks.dtype),
            jax.ShapeDtypeStruct((STEPS, groups, slots, width, width), blocks.dtype),
            jax.ShapeDtypeStruct((STEPS,) + meta.shape, meta.dtype),
            jax.ShapeDtypeStruct((STEPS,) + meta.shape, meta.dtype),
        ),
        in_specs=[pl.BlockSpec(memory_space=pl.ANY), vmem],
        out_specs=(vmem, vmem, vmem, vmem),
        scratch_shapes=[
            pltpu.SemaphoreType.DMA(((3 + groups) * STEPS,)),
            pltpu.SemaphoreType.DMA(((3 + groups) * STEPS,)),
        ],
        compiler_params=pltpu.CompilerParams(collective_id=0, has_side_effects=True),
    )(blocks, meta)


def trace_kernel(row_count, col_count, groups, scale_width,
                 term_ref, out_ref, row_buf, col_buf, send_sem, recv_sem, col_send, col_recv):
    r = lax.axis_index("row")
    c = lax.axis_index("col")
    diagonal = c == r // groups
    barrier = pltpu.get_barrier_semaphore()

    @pl.when(diagonal)
    def _():
        for cc in range(col_count):
            @pl.when(cc != c)
            def _(cc=cc):
                pl.semaphore_signal(barrier, 1, device_id=(r, cc), device_id_type=MESH)

    @pl.when(jnp.logical_not(diagonal))
    def _():
        pl.semaphore_signal(barrier, 1, device_id=(r, r // groups), device_id_type=MESH)

    for rr in range(row_count):
        @pl.when(rr != r)
        def _(rr=rr):
            pl.semaphore_signal(barrier, 1, device_id=(rr, c), device_id_type=MESH)

    pl.semaphore_wait(barrier, (row_count - 1) + jnp.where(diagonal, col_count - 1, 1))

    row_copies = []
    for cc in range(col_count):
        row_copies.append(pltpu.make_async_remote_copy(
            term_ref, row_buf, send_sem.at[cc], recv_sem.at[0],
            device_id=(r, cc), device_id_type=MESH,
        ))

    @pl.when(diagonal)
    def _():
        for cc in range(col_count):
            @pl.when(cc != c)
            def _(cc=cc):
                row_copies[cc].start()

    @pl.when(jnp.logical_not(diagonal))
    def _():
        row_copies[0].wait_recv()

    def col_copy(source, rr):
        return pltpu.make_async_remote_copy(
            source, col_buf.at[r], col_send.at[rr], col_recv.at[r],
            device_id=(rr, c), device_id_type=MESH,
        )

    for source, chosen in ((term_ref, diagonal), (row_buf, jnp.logical_not(diagonal))):
        @pl.when(chosen)
        def _(source=source):
            for rr in range(row_count):
                @pl.when(rr != r)
                def _(rr=rr):
                    col_copy(source, rr).start()

    for rr in range(row_count):
        @pl.when(rr != r)
        def _(rr=rr):
            pltpu.make_async_remote_copy(
                term_ref, col_buf.at[rr], col_send.at[rr], col_recv.at[rr],
                device_id=(rr, c), device_id_type=MESH,
            ).wait_recv()

    for source, chosen in ((term_ref, diagonal), (row_buf, jnp.logical_not(diagonal))):
        @pl.when(chosen)
        def _(source=source):
            for rr in range(row_count):
                @pl.when(rr != r)
                def _(rr=rr):
                    col_copy(source, rr).wait_send()
            col_buf[r] = source[...]

    @pl.when(diagonal)
    def _():
        for cc in range(col_count):
            @pl.when(cc != c)
            def _(cc=cc):
                row_copies[cc].wait_send()

    total = jnp.zeros(col_buf.shape[1:], jnp.float32)
    for rr in range(row_count):
        total = total + col_buf[rr]
    out_ref[...] = total[0:1, 0:1] / math.sqrt(row_count * RB * scale_width)


def trace_total(term, row_count, col_count, groups, width):
    tile = term.reshape(1, 1)
    vmem = pl.BlockSpec(memory_space=pltpu.VMEM)
    out = pl.pallas_call(
        functools.partial(trace_kernel, row_count, col_count, groups, width),
        out_shape=jax.ShapeDtypeStruct((1, 1), jnp.float32),
        in_specs=[vmem],
        out_specs=vmem,
        scratch_shapes=[
            pltpu.VMEM((1, 1), jnp.float32),
            pltpu.VMEM((row_count, 1, 1), jnp.float32),
            pltpu.SemaphoreType.DMA((col_count,)),
            pltpu.SemaphoreType.DMA((1,)),
            pltpu.SemaphoreType.DMA((row_count,)),
            pltpu.SemaphoreType.DMA((row_count,)),
        ],
        compiler_params=pltpu.CompilerParams(collective_id=1, has_side_effects=True),
    )(tile)
    return out.reshape(())


def body(blocks, block_rows, block_cols, counts):
    groups = blocks.shape[2]
    slot_count = blocks.shape[3]
    width = blocks.shape[4]
    row_count = lax.axis_size("row")
    col_count = lax.axis_size("col")
    row_place = lax.axis_index("row")
    col_place = lax.axis_index("col")
    lower = row_place % groups
    filled = counts[0, 0]
    live = jnp.arange(slot_count, dtype=jnp.int32)[None, :] < filled[:, None]
    left_places_all = jnp.where(live, block_rows[0, 0] * RB + block_cols[0, 0], -1)
    offsets = (jnp.arange(groups, dtype=jnp.int32) * RB)[:, None]
    right_places = jnp.where(
        live, block_rows[0, 0] * (groups * RB) + block_cols[0, 0] + offsets, -1
    ).reshape(-1)
    left_places = lax.dynamic_index_in_dim(left_places_all, lower, 0, keepdims=False)
    meta = jnp.stack([
        jnp.pad(left_places, (0, (groups - 1) * slot_count)),
        right_places,
    ])
    recv_l, recv_r, recv_ml, recv_mr = exchange(blocks[0, 0], meta, row_count, col_count)
    totals = jnp.zeros((RB * width, groups * RB * width), jnp.float32)
    for step in range(STEPS):
        rp = recv_r[step].reshape(groups * slot_count, width, width)
        right_dense = densify(rp, recv_mr[step, 1, : groups * slot_count], RB, groups * RB)
        left_dense = densify(recv_l[step], recv_ml[step, 0, :slot_count], RB, RB)
        totals = totals + jnp.dot(left_dense, right_dense, preferred_element_type=jnp.float32)
    shift_amount = row_place - groups * col_place
    valid = (shift_amount >= 0) & (shift_amount < groups)
    start = jnp.clip(shift_amount, 0, groups - 1) * RB * width
    window = lax.dynamic_slice_in_dim(totals, start, RB * width, 1)
    term = jnp.where(valid, jnp.trace(window), jnp.zeros((), jnp.float32))
    trace_value = trace_total(term, row_count, col_count, groups, width)
    return (totals.astype(jnp.bfloat16), trace_value)


def solution(mesh):
    return jax.shard_map(
        body,
        mesh=mesh,
        in_specs=(
            P("row", "col", None, None, None, None),
            P("row", "col", None, None),
            P("row", "col", None, None),
            P("row", "col", None),
        ),
        out_specs=(P("row", "col"), P()),
        check_vma=False,
    )
```
